128 devices in a mesh: tile: 16 (over x, z), dp: 8 (over y, core).
Axes of the slice: x: 4, y: 4, z: 4, core: 2. Of those that a mesh axis runs over, the one named last changes fastest.
Arguments:
- features: bfloat16 [1024, 256, 128], P('tile'), may hold values from -6 to 6
- target_field: bfloat16 [1024, 256], P('tile'), may hold values from -3 to 3
- owner_tile: int32 [512, 1], P(('tile', 'dp')), may hold values from 0 to 15; in each aligned block of 4 rows (0 to 3, 4 to 7, ...) at most 2 rows name the same one
- row_offset: int32 [512], P(('tile', 'dp')), may hold values from 0 to 48
- column_start: int32 [512], P(('tile', 'dp')), may hold values from 0 to 240
- noise_level: int32 [512], P(('tile', 'dp')), may hold values from 0 to 31
- icing_count: int32 [512], P(('tile', 'dp')), may hold values from 1 to 4
- noise_draw: float32 [512, 16, 16], P(('tile', 'dp')), may hold values from -6 to 6
- w_a: bfloat16 [1152, 512], replicated, may hold values from -0.1875 to 0.1875
- w_u: float32 [9, 512], replicated, may hold values from -2 to 2
- b_a: float32 [512], replicated, may hold values from -3 to 3
- e_a: float32 [512], replicated, may hold values from -6 to 6
- w_b: bfloat16 [4608, 128], replicated, may hold values from -0.09375 to 0.09375
- b_b: float32 [128], replicated, may hold values from -3 to 3
- w_o: float32 [128], replicated, may hold values from -0.5 to 0.5
Outputs:
- losses: float32 [512], P(('tile', 'dp'))
- upd_a: float32 [512, 1152], P(('tile', 'dp'))
- upd_b: float32 [512, 1152], P(('tile', 'dp'))
The draws below stay inside these ranges and needn't reach their ends.
Inputs may be any that keep to these rules, and one draw needn't show every extreme that they name: `owner_tile`: among the 4 patches of one device no tile is named more than 2 times, a bound that some block reaches. `row_offset`: a patch's rows lie inside its tile.
All inputs are finite; a program needn't handle non-finite values.
Results may differ from the reference program's by a relative error of at most 0.0027.
Values may be sent and summed in bfloat16 or wider, within the bound.
A program may use at most 128 MiB of HBM per device.

```python
import math
import jax
import jax.numpy as jnp
import numpy as np
from jax import lax

C = 128
HID = 512
P_SIZE = 16
LEVELS = 32
PATCH_DEV = 4
TILE_ROWS = 64
W = 256
CAP = 2
GRID_ROWS = 1024
PATCHES = 512
N_TILE = 16


def place_ends(array, key, low, high):
    shape = array.shape
    spot = [jax.random.randint(jax.random.fold_in(key, axis), (), 0, shape[axis]) for axis in range(len(shape))]
    array = array.at[tuple(spot)].set(low)
    longest = shape.index(max(shape))
    spot[longest] = (spot[longest] + 1) % shape[longest]
    return array.at[tuple(spot)].set(high)


def levels(stream_key, dims, cuts, least, largest):
    gain, own = 1.0, jax.random.fold_in(stream_key, 6)
    for axis_at, shards_of in cuts:
        draws = jnp.exp(jax.random.uniform(jax.random.fold_in(own, axis_at), (shards_of,), jnp.float32, least / len(cuts), largest / len(cuts)))
        gain = gain * jnp.repeat(draws, dims[axis_at] // shards_of).reshape([-1 if axis == axis_at else 1 for axis in range(len(dims))])
    return gain


def routed_block(own_key, own, number, rows, amount, top, reach, skew):
    order = jax.random.permutation(own_key, amount)
    packed, common = load_shares(amount, rows * top, reach, skew, True), load_shares(amount, rows * top, reach, skew, False)
    places = jnp.arange(amount)

    def named(lengths, turn):
        used = int((lengths > 0).sum())
        fixed = max(1, used // 4)
        passed = fixed + (places - fixed + turn * (used - fixed)) % max(1, amount - fixed)
        return jnp.zeros((amount,), jnp.int32).at[order[jnp.where(places < fixed, places, passed)]].set(jnp.asarray(lengths, jnp.int32))

    lengths = jnp.where(number % 4 == 0, named(packed, number // 4), named(common, number - number // 4 - 1))
    mixed = jax.random.permutation(jax.random.fold_in(own, 3), amount)
    source_of, taker = mixed[0:amount // 2 * 2:2], mixed[1:amount // 2 * 2:2]
    slack = jnp.minimum(lengths[source_of] - 1, reach - lengths[taker]) // 2
    slack = jnp.where((source_of == order[0]) | (taker == order[0]) | (lengths[taker] == 0), 0, jnp.maximum(slack, 0))
    passed = jax.random.randint(jax.random.fold_in(own, 4), (amount // 2,), 0, 1 << 20) % (slack + 1)
    lengths = lengths.at[source_of].add(-passed).at[taker].add(passed)
    labels = jnp.searchsorted(jnp.cumsum(lengths), jnp.arange(rows * top), side="right").astype(jnp.int32)
    grid = labels.reshape(top, rows).T
    grid = grid[jax.random.permutation(jax.random.fold_in(own, 1), rows)]
    turn = jax.random.randint(jax.random.fold_in(own, 2), (rows, 1), 0, top)
    return jnp.take_along_axis(grid, (jnp.arange(top)[None, :] + turn) % top, axis=1)


def load_shares(amount, total, reach, skew, full):
    weights = [(1 << 20) // math.isqrt(grade ** skew) + 1 for grade in range(1, amount + 1)]
    largest = reach if full else min(reach, max(-(-total // amount), total * weights[0] // sum(weights)))
    least = 1 if total - largest >= amount - 1 else 0
    given, spare = [largest] + [least] * (amount - 1), total - largest - least * (amount - 1)
    while spare > 0:
        movable = [i for i in range(1, amount) if given[i] < largest] or [i for i in range(1, amount) if given[i] < reach]
        mass, budget = sum([weights[i] for i in movable]), spare
        for i in movable:
            addition = min(reach - given[i], max(1, budget * weights[i] // mass), spare)
            given[i] = given[i] + addition
            spare = spare - addition
    return np.array(given)


def scatter_about(own_key, extent, scale, limit, cuts=(), kind=jnp.bfloat16):
    level = levels(own_key, extent, cuts, -0.22, 0.18) if cuts else 1.0
    drawn = jax.random.normal(own_key, extent, jnp.float32) * scale * level
    return jnp.minimum(jnp.maximum(drawn, -limit), limit).astype(kind)


def setup_inputs(seed: int = 0) -> dict:
    keys = jax.random.split(jax.random.key(seed), 16)
    features = scatter_about(keys[0], (GRID_ROWS, W, C), 1.0, 6.0, ((0, 16),))
    target_field = scatter_about(keys[1], (GRID_ROWS, W), 0.5, 3.0, ((0, 16),))
    owner_tile_keys = jax.random.split(jax.random.fold_in(keys[2], 1), PATCHES // PATCH_DEV)
    owner_tile_turns = jax.random.permutation(jax.random.fold_in(keys[2], 3), PATCHES // PATCH_DEV)
    owner_tile = jax.vmap(lambda own, number: routed_block(jax.random.fold_in(keys[2], 2), own, number, PATCH_DEV, N_TILE, 1, CAP, 2))(owner_tile_keys, owner_tile_turns).reshape((PATCHES, 1))
    row_offset = place_ends(jax.random.randint(keys[3], (PATCHES,), 0, TILE_ROWS - P_SIZE + 1), jax.random.fold_in(keys[3], 1), 0, TILE_ROWS - P_SIZE).astype(jnp.int32)
    column_start = place_ends(jax.random.randint(keys[4], (PATCHES,), 0, W - P_SIZE + 1), jax.random.fold_in(keys[4], 1), 0, W - P_SIZE).astype(jnp.int32)
    noise_level = place_ends(jax.random.randint(keys[5], (PATCHES,), 0, LEVELS), jax.random.fold_in(keys[5], 1), 0, LEVELS - 1).astype(jnp.int32)
    icing_count = place_ends(jax.random.randint(keys[6], (PATCHES,), 1, 5), jax.random.fold_in(keys[6], 1), 1, 4).astype(jnp.int32)
    noise_draw = scatter_about(keys[7], (PATCHES, P_SIZE, P_SIZE), 1.0, 6.0, ((0, 128),), jnp.float32)
    w_a = scatter_about(keys[8], (9 * C, HID), (9 * C) ** -0.5, 0.1875)
    w_u = scatter_about(keys[9], (9, HID), 9 ** -0.5, 2.0, (), jnp.float32)
    b_a = scatter_about(keys[10], (HID,), 0.5, 3.0, (), jnp.float32)
    e_a = scatter_about(keys[11], (HID,), 1.0, 6.0, (), jnp.float32)
    w_b = scatter_about(keys[12], (9 * HID, C), (9 * HID) ** -0.5, 0.09375)
    b_b = scatter_about(keys[13], (C,), 0.5, 3.0, (), jnp.float32)
    w_o = scatter_about(keys[14], (C,), C ** -0.5, 0.5, (), jnp.float32)
    return {"features": features, "target_field": target_field, "owner_tile": owner_tile, "row_offset": row_offset, "column_start": column_start, "noise_level": noise_level, "icing_count": icing_count, "noise_draw": noise_draw, "w_a": w_a, "w_u": w_u, "b_a": b_a, "e_a": e_a, "w_b": w_b, "b_b": b_b, "w_o": w_o}


SIGMA_LOW = 0.02
SIGMA_HIGH = 80.0
SIGMA_DATA = 0.5
EPSILON = 1e-06

def silu_prime(values):
    sigmoid_val = jax.nn.sigmoid(values)
    return sigmoid_val * (1.0 + values * (1.0 - sigmoid_val))

def tap_window(padded, shift_row, shift_col, side_len):
    window = padded[:, shift_row:shift_row + side_len, shift_col:shift_col + side_len]
    return window.reshape((-1,) + padded.shape[3:])

def patch_terms(patch_feats, patch_target, noise_draw, noise_level, icing_count, w_a, w_u, b_a, e_a, w_b, b_b, w_o):
    npatch = patch_feats.shape[0]
    side_len = patch_feats.shape[1]
    channels = patch_feats.shape[3]
    hidden_width = w_a.shape[1]
    pixels = side_len * side_len
    log_step = (math.log(SIGMA_HIGH) - math.log(SIGMA_LOW)) / (LEVELS - 1)
    sigmas = jnp.exp(math.log(SIGMA_LOW) + noise_level.astype(jnp.float32) * log_step)
    variance = sigmas * sigmas + SIGMA_DATA * SIGMA_DATA
    scale_in = 1.0 / jnp.sqrt(variance)
    scale_skip = SIGMA_DATA * SIGMA_DATA / variance
    scale_out = sigmas * SIGMA_DATA * scale_in
    noise_embed = jnp.log(sigmas) / 4.0
    clean_field = patch_target.astype(jnp.float32)
    noisy_field = clean_field + sigmas[:, None, None] * noise_draw
    aim_value = ((clean_field - scale_skip[:, None, None] * noisy_field) / scale_out[:, None, None]).reshape(-1)
    scaled_in = jnp.pad(scale_in[:, None, None] * noisy_field, ((0, 0), (1, 1), (1, 1)))
    feat_pad = jnp.pad(patch_feats, ((0, 0), (1, 1), (1, 1), (0, 0)))
    embed_rows = jnp.repeat(noise_embed, pixels)
    pre_a = b_a[None, :] + embed_rows[:, None] * e_a[None, :]
    for tap_index in range(9):
        shift_row, shift_col = (tap_index // 3, tap_index % 3)
        window = tap_window(feat_pad, shift_row, shift_col, side_len)
        pre_a = pre_a + jnp.dot(window, w_a[tap_index * channels:(tap_index + 1) * channels], preferred_element_type=jnp.float32)
        pre_a = pre_a + tap_window(scaled_in, shift_row, shift_col, side_len)[:, None] * w_u[tap_index][None, :]
    hidden_act = jax.nn.silu(pre_a).astype(jnp.bfloat16)
    act_pad = jnp.pad(hidden_act.reshape(npatch, side_len, side_len, hidden_width), ((0, 0), (1, 1), (1, 1), (0, 0)))
    pre_b = jnp.zeros((npatch * pixels, channels), jnp.float32) + b_b[None, :]
    for tap_index in range(9):
        shift_row, shift_col = (tap_index // 3, tap_index % 3)
        window = tap_window(act_pad, shift_row, shift_col, side_len)
        pre_b = pre_b + jnp.dot(window, w_b[tap_index * hidden_width:(tap_index + 1) * hidden_width], preferred_element_type=jnp.float32)
    out_act = jax.nn.silu(pre_b)
    output_map = jnp.dot(out_act, w_o, precision=lax.Precision.HIGHEST)
    residual = output_map - aim_value
    weights = jnp.repeat(icing_count.astype(jnp.float32), pixels)
    losses = lax.optimization_barrier(jnp.mean((weights * residual * residual).reshape(npatch, pixels), axis=1))
    grad_final = 2.0 * weights * residual / pixels
    grad_pre_b = (grad_final[:, None] * w_o[None, :] * silu_prime(pre_b)).astype(jnp.bfloat16)
    grad_hidden = jnp.zeros((npatch, side_len + 2, side_len + 2, hidden_width), jnp.float32)
    parts_b = []
    for tap_index in range(9):
        shift_row, shift_col = (tap_index // 3, tap_index % 3)
        window = tap_window(act_pad, shift_row, shift_col, side_len)
        parts_b.append(lax.dot_general(window, grad_pre_b, (((0,), (0,)), ((), ())), preferred_element_type=jnp.float32))
        back_term = lax.dot_general(grad_pre_b, w_b[tap_index * hidden_width:(tap_index + 1) * hidden_width], (((1,), (1,)), ((), ())), preferred_element_type=jnp.float32)
        grad_hidden = grad_hidden.at[:, shift_row:shift_row + side_len, shift_col:shift_col + side_len].add(back_term.reshape(npatch, side_len, side_len, hidden_width))
    grad_pre_a = (grad_hidden[:, 1:-1, 1:-1].reshape(-1, hidden_width) * silu_prime(pre_a)).astype(jnp.bfloat16)
    parts_a = []
    for tap_index in range(9):
        shift_row, shift_col = (tap_index // 3, tap_index % 3)
        window = tap_window(feat_pad, shift_row, shift_col, side_len)
        parts_a.append(lax.dot_general(grad_pre_a, window, (((0,), (0,)), ((), ())), preferred_element_type=jnp.float32))
    return (losses, jnp.concatenate(parts_a, axis=1), jnp.concatenate(parts_b, axis=1))

def reference(features, target_field, owner_tile, row_offset, column_start, noise_level, icing_count, noise_draw, w_a, w_u, b_a, e_a, w_b, b_b, w_o):
    total_patches = owner_tile.shape[0]
    group_size = min(total_patches, PATCH_DEV * 8)
    groups = total_patches // group_size
    grid_row = (owner_tile[:, 0] * TILE_ROWS + row_offset).astype(jnp.int32)

    def extract(source_row, source_col):
        anchor = jnp.zeros((), jnp.int32)
        feat_block = lax.dynamic_slice(features, (source_row, source_col, anchor), (P_SIZE, P_SIZE, C))
        target_block = lax.dynamic_slice(target_field, (source_row, source_col), (P_SIZE, P_SIZE))
        return (feat_block, target_block)

    def one_group(totals, inputs):
        rows_in, cols_in, levels_in, counts_in, noise_in = inputs
        blocks, fields = jax.vmap(extract)(rows_in, cols_in)
        group_losses, part_a, part_b = patch_terms(blocks, fields, noise_in, levels_in, counts_in, w_a, w_u, b_a, e_a, w_b, b_b, w_o)
        return ((totals[0] + part_a, totals[1] + part_b), group_losses)
    inputs = (grid_row.reshape(groups, group_size), column_start.astype(jnp.int32).reshape(groups, group_size), noise_level.reshape(groups, group_size), icing_count.reshape(groups, group_size), noise_draw.reshape(groups, group_size, P_SIZE, P_SIZE))
    start_sum = (jnp.zeros((HID, 9 * C), jnp.float32), jnp.zeros((HID, 9 * C), jnp.float32))
    (grad_a, grad_b), losses = lax.scan(one_group, start_sum, inputs)
    upd_a = grad_a / jnp.sqrt(jnp.mean(grad_a * grad_a) + EPSILON)
    upd_b = grad_b / jnp.sqrt(jnp.mean(grad_b * grad_b) + EPSILON)
    return (losses.reshape(-1), upd_a, upd_b)
```

```python
import functools
import math

import jax
import jax.numpy as jnp
from jax import lax
from jax.experimental import pallas as pl
from jax.experimental.pallas import tpu as pltpu
from jax.sharding import PartitionSpec as P

C = 128
HID = 512
SIDE = 16
LEVELS = 32
NP = 4
CELLS = SIDE * SIDE
TAPS = 9
WIDE = TAPS * C
SIGMA_LOW = 0.02
SIGMA_HIGH = 80.0
SIGMA_DATA = 0.5
EPSILON = 1e-06
LOG_LOW = math.log(SIGMA_LOW)
LOG_STEP = (math.log(SIGMA_HIGH) - math.log(SIGMA_LOW)) / (LEVELS - 1)

MESH = pl.DeviceIdType.MESH
F32 = jnp.float32
BF16 = jnp.bfloat16
N_TILE = 16
N_DP = 8
AX = 4
PART = WIDE // 3


def iota(shape, dim):
    return lax.broadcasted_iota(jnp.int32, shape, dim)


def remote(src, dst, send_sem, recv_sem, tile, dp):
    return pltpu.make_async_remote_copy(
        src_ref=src,
        dst_ref=dst,
        send_sem=send_sem,
        recv_sem=recv_sem,
        device_id=(tile, dp),
        device_id_type=MESH,
    )


def column_shifts(block):
    col = iota(block.shape, 1)
    before = jnp.where(col == 0, 0.0, pltpu.roll(block, 1, axis=1))
    after = jnp.where(col == SIDE - 1, 0.0, pltpu.roll(block, SIDE - 1, axis=1))
    return before, block, after


def store_rows(dst, p, lane, rows, delta):
    lanes = slice(lane, lane + C)
    base = p * SIDE
    zero = jnp.zeros((1, SIDE, C), BF16)
    if delta == 0:
        dst[base : base + SIDE, :, lanes] = rows
    elif delta < 0:
        dst[base : base + 1, :, lanes] = zero
        dst[base + 1 : base + SIDE, :, lanes] = rows[: SIDE - 1]
    else:
        dst[base : base + SIDE - 1, :, lanes] = rows[1:]
        dst[base + SIDE - 1 : base + SIDE, :, lanes] = zero


def kernel(
    feat_hbm,
    tgt_ref,
    owner_ref,
    row_ref,
    col_ref,
    level_ref,
    count_ref,
    noise_ref,
    wa_hbm,
    wu_ref,
    ba_ref,
    ea_ref,
    wb_hbm,
    bb_ref,
    wo_ref,
    losses_ref,
    upda_ref,
    updb_ref,
    feat_v,
    feat_f,
    tgt_v,
    req_send,
    req_recv,
    req_smem,
    slots,
    landed,
    blk,
    noise_v,
    wfull,
    wext,
    w2,
    xcol,
    gcol,
    act,
    slope,
    gpa,
    mine,
    theirs,
    sib_recv,
    s1_send,
    s1_recv,
    s2_send,
    s2_recv,
    s3_send,
    s3_recv,
    fin_send,
    fin_recv,
    nrm_send,
    nrm_recv,
    nrm2_send,
    nrm2_recv,
    local_sem,
    req_ssem,
    req_rsem,
    slot_ssem,
    slot_rsem,
    sib_sem,
    s1_ssem,
    s1_rsem,
    s2_ssem,
    s2_rsem,
    s3_ssem,
    s3_rsem,
    fin_sem,
    n1_ssem,
    n1_rsem,
    n2_ssem,
    n2_rsem,
):
    me_t = lax.axis_index("tile")
    me_d = lax.axis_index("dp")
    x, z = me_t // AX, me_t % AX
    y, core = me_d // 2, me_d % 2

    def tile_peer(o):
        return ((x + o // AX) % AX) * AX + (z + o % AX) % AX

    def dp_peer(o):
        return (me_d + o) % N_DP

    barrier = pltpu.get_barrier_semaphore()

    @pl.loop(1, N_TILE)
    def _(o):
        pl.semaphore_signal(barrier, inc=1, device_id=(tile_peer(o), me_d), device_id_type=MESH)

    @pl.loop(1, N_DP)
    def _(o):
        pl.semaphore_signal(barrier, inc=1, device_id=(me_t, dp_peer(o)), device_id_type=MESH)

    feat_copy = pltpu.make_async_copy(feat_hbm, feat_v, local_sem.at[0])
    feat_copy.start()
    wa_copy = pltpu.make_async_copy(wa_hbm, wfull.at[pl.ds(0, WIDE)], local_sem.at[1])
    wa_copy.start()
    wb_copies = [
        pltpu.make_async_copy(
            wb_hbm.at[pl.ds(t * HID, HID)], w2.at[:, pl.ds(t * C, C)], local_sem.at[2 + t]
        )
        for t in range(TAPS)
    ]
    for copy in wb_copies:
        copy.start()

    lane = iota((1, C), 1)
    line = jnp.zeros((1, C), jnp.int32)
    for k in range(NP):
        line = jnp.where(lane == 4 * k, owner_ref[k, 0], line)
        line = jnp.where(lane == 4 * k + 1, row_ref[k], line)
        line = jnp.where(lane == 4 * k + 2, col_ref[k], line)
    req_send[...] = line
    req_recv[me_t] = line
    tgt_v[0] = tgt_ref[:, :C].astype(F32)
    tgt_v[1] = tgt_ref[:, C:].astype(F32)
    pl.semaphore_wait(barrier, N_TILE - 1 + N_DP - 1)

    def req_copy(o):
        return remote(
            req_send, req_recv.at[me_t], req_ssem.at[o], req_rsem.at[o], tile_peer(o), me_d
        )

    @pl.loop(1, N_TILE)
    def _(o):
        req_copy(o).start()

    feat_copy.wait()

    @pl.loop(0, 64)
    def _(i):
        feat_f[i] = feat_v[i].astype(F32)

    @pl.loop(1, N_TILE)
    def _(o):
        req_copy(o).wait()

    to_smem = pltpu.make_async_copy(req_recv, req_smem, local_sem.at[2 + TAPS])
    to_smem.start()
    to_smem.wait()

    def cut(row, col):
        block = feat_f[pl.ds(row, SIDE), pl.ds(col, SIDE), :]
        rows = jnp.concatenate([tgt_v[i, pl.ds(row, SIDE), :] for i in range(2)], axis=1)
        shift = jnp.full(rows.shape, col, jnp.int32)
        for bit in (1, 2, 4, 8, 16, 32, 64, 128):
            rows = jnp.where((shift & bit) != 0, pltpu.roll(rows, 256 - bit, axis=1), rows)
        return block.astype(BF16), rows[:, :C].astype(BF16)

    def fill(dst, j):
        rank = jnp.int32(0)
        rows = [jnp.int32(0), jnp.int32(0)]
        cols = [jnp.int32(0), jnp.int32(0)]
        for k in range(NP):
            hit = req_smem[j, 0, 4 * k] == me_t
            for q in range(2):
                take = hit & (rank == q)
                rows[q] = jnp.where(take, req_smem[j, 0, 4 * k + 1], rows[q])
                cols[q] = jnp.where(take, req_smem[j, 0, 4 * k + 2], cols[q])
            rank = rank + hit.astype(jnp.int32)
        for q in range(2):
            block, field = cut(rows[q], cols[q])
            dst[q, :SIDE] = block
            dst[q, SIDE] = field

    def slot_copy(o):
        return remote(
            slots.at[o], landed.at[me_t], slot_ssem.at[o], slot_rsem.at[o], tile_peer(o), me_d
        )

    @pl.loop(1, N_TILE)
    def _(i):
        o = (i * 5) % N_TILE
        fill(slots.at[o], tile_peer(o))
        slot_copy(o).start()

    fill(landed.at[me_t], me_t)

    wa_copy.wait()
    for copy in wb_copies:
        copy.wait()
    wu = wu_ref[...]
    wu_hi = wu.astype(BF16).astype(F32)
    ba = ba_ref[...].reshape(1, HID)
    ba_hi = ba.astype(BF16).astype(F32)
    ea = ea_ref[...].reshape(1, HID)
    ea_hi = ea.astype(BF16).astype(F32)
    wext[...] = jnp.zeros_like(wext)
    wext[0:9] = wu_hi
    wext[9:18] = wu - wu_hi
    wext[18:27] = wu_hi
    wext[27:28] = ba_hi
    wext[28:29] = ba - ba_hi
    wext[29:30] = ea_hi
    wext[30:31] = ea - ea_hi
    wext[31:32] = ea_hi
    wfull[WIDE:, :] = wext[...].astype(BF16)
    noise_v[...] = jnp.zeros_like(noise_v)
    noise_v[:, :, 0:SIDE] = noise_ref[...]

    @pl.loop(1, N_TILE)
    def _(o):
        slot_copy(o).wait()

    owners = [owner_ref[k, 0] for k in range(NP)]
    for k in range(NP):
        rank = jnp.int32(0)
        for before in range(k):
            rank = rank + (owners[before] == owners[k]).astype(jnp.int32)
        blk[k] = landed[owners[k], jnp.minimum(rank, 1)]

    wo = wo_ref[...].reshape(1, 1, C)
    bb = bb_ref[...].reshape(1, 1, C)
    shape3 = (SIDE, SIDE, C)
    col3, lane3 = iota(shape3, 1), iota(shape3, 2)
    lane2 = iota((SIDE, C), 1)
    for p in range(NP):
        block = blk[p, :SIDE].astype(F32)
        for s, moved in enumerate(column_shifts(block)):
            rows = moved.astype(BF16)
            for r in range(3):
                store_rows(xcol, p, (3 * r + s) * C, rows, r - 1)

        level = jnp.full((SIDE, C), level_ref[p], jnp.int32).astype(F32)
        sigma = jnp.exp(LOG_LOW + level * LOG_STEP)
        variance = sigma * sigma + SIGMA_DATA * SIGMA_DATA
        scale_in = 1.0 / jnp.sqrt(variance)
        scale_skip = SIGMA_DATA * SIGMA_DATA / variance
        scale_out = sigma * SIGMA_DATA * scale_in
        embed = jnp.log(sigma) / 4.0
        clean = jnp.where(lane2 < SIDE, blk[p, SIDE].astype(F32), 0.0)
        noisy = clean + sigma * noise_v[p]
        aim = (clean - scale_skip * noisy) / scale_out
        scaled = pltpu.roll(scale_in * noisy, 1, axis=1)
        wide = jnp.broadcast_to(scaled[:, None, :], shape3)
        for bit in (1, 2, 4, 8):
            wide = jnp.where((col3 & bit) != 0, pltpu.roll(wide, C - bit, axis=2), wide)
        wide = jnp.where(lane3 < 3, wide, 0.0)
        none = jnp.zeros((1, SIDE, C), F32)
        taps = (
            jnp.concatenate([none, wide[: SIDE - 1]], axis=0)
            + pltpu.roll(wide, 3, axis=2)
            + pltpu.roll(jnp.concatenate([wide[1:], none], axis=0), 6, axis=2)
        )
        taps_hi = taps.astype(BF16).astype(F32)
        emb = embed[0:1, :][None]
        emb_hi = emb.astype(BF16).astype(F32)
        extra = taps_hi + pltpu.roll(taps_hi, 9, axis=2) + pltpu.roll(taps - taps_hi, 18, axis=2)
        extra = jnp.where((lane3 == 27) | (lane3 == 28), 1.0, extra)
        extra = jnp.where((lane3 == 29) | (lane3 == 30), emb_hi, extra)
        extra = jnp.where(lane3 == 31, emb - emb_hi, extra)
        xcol[p * SIDE : (p + 1) * SIDE, :, WIDE:] = extra.astype(BF16)

        cells = slice(p * CELLS, (p + 1) * CELLS)
        window = xcol[p * SIDE : (p + 1) * SIDE].reshape(CELLS, WIDE + C)
        pre_a = jnp.dot(window, wfull[...], preferred_element_type=F32)
        gate = jax.nn.sigmoid(pre_a)
        slope[cells] = gate * (1.0 + pre_a * (1.0 - gate))
        hidden = (pre_a * gate).astype(BF16)
        act[cells] = hidden

        spread = jnp.dot(hidden, w2[...], preferred_element_type=F32).reshape(SIDE, SIDE, WIDE)

        def tap_rows(s):
            up = spread[:, :, s * C : (s + 1) * C]
            mid = spread[:, :, (3 + s) * C : (4 + s) * C]
            down = spread[:, :, (6 + s) * C : (7 + s) * C]
            return (
                mid
                + jnp.concatenate([none, up[: SIDE - 1]], axis=0)
                + jnp.concatenate([down[1:], none], axis=0)
            )

        left = jnp.where(col3 == 0, 0.0, pltpu.roll(tap_rows(0), 1, axis=1))
        right = jnp.where(col3 == SIDE - 1, 0.0, pltpu.roll(tap_rows(2), SIDE - 1, axis=1))
        pre_b = bb + tap_rows(1) + left + right
        gate_b = jax.nn.sigmoid(pre_b)
        aim3 = jnp.where(col3 == lane3, jnp.broadcast_to(aim[:, None, :], shape3), 0.0)
        residual = jnp.sum(pre_b * gate_b * wo - aim3, axis=2, keepdims=True)
        weight = count_ref[p].astype(F32)
        losses_ref[p] = jnp.sum(residual * residual) * weight / CELLS
        grad_final = (2.0 * weight / CELLS) * residual
        grad_b = grad_final * wo * (gate_b * (1.0 + pre_b * (1.0 - gate_b)))
        grad_b = grad_b.astype(BF16).astype(F32)
        for s, moved in enumerate(column_shifts(grad_b)):
            rows = moved.astype(BF16)
            for r in range(3):
                store_rows(gcol, p, (3 * (2 - r) + (2 - s)) * C, rows, r - 1)

        back = lax.dot_general(
            gcol[p * SIDE : (p + 1) * SIDE].reshape(CELLS, WIDE),
            w2[...],
            (((1,), (1,)), ((), ())),
            preferred_element_type=F32,
        )
        gpa[cells] = (back * slope[cells]).astype(BF16)

    over_cells = (((0,), (0,)), ((), ()))
    for part in range(3):
        lanes = slice(part * PART, (part + 1) * PART)
        grad_a = lax.dot_general(
            gpa[...],
            xcol[:, :, lanes].reshape(NP * CELLS, PART),
            over_cells,
            preferred_element_type=F32,
        )
        grad_b = lax.dot_general(
            act[...],
            gcol[:, :, lanes].reshape(NP * CELLS, PART),
            over_cells,
            preferred_element_type=F32,
        )
        first = core == 0
        mine[:, lanes] = jnp.where(first, grad_a, grad_b)
        theirs[:, lanes] = jnp.where(first, grad_b, grad_a)

    sib = me_d + 1 - 2 * core
    sib_copy = remote(theirs, sib_recv, sib_sem.at[0], sib_sem.at[1], me_t, sib)
    sib_copy.start()
    sib_copy.wait()
    mine[...] = mine[...] + sib_recv[...]

    def along(axis, o):
        if axis == 0:
            at = (x + o) % AX
            return at * AX + z, me_d, at
        if axis == 1:
            at = (z + o) % AX
            return x * AX + at, me_d, at
        at = (y + o) % AX
        return me_t, at * 2 + core, at

    here = (x, z, y)
    orders = ((0, 1, 2), (1, 2, 0), (2, 0, 1))

    def step1_part(part, at):
        lanes = slice(part * PART, (part + 1) * PART)
        if part == 0:
            return mine[pl.ds(pl.multiple_of(at * 128, 128), 128), lanes].reshape(16, 8, PART)
        if part == 1:
            return jnp.concatenate(
                [
                    mine[pl.ds(pl.multiple_of(i * 128 + at * 32, 32), 32), lanes].reshape(4, 8, PART)
                    for i in range(4)
                ],
                axis=0,
            )
        return jnp.concatenate(
            [
                mine[pl.ds(pl.multiple_of(i * 32 + at * 8, 8), 8), lanes].reshape(1, 8, PART)
                for i in range(16)
            ],
            axis=0,
        )

    copies = []
    for o in (2, 1, 3):
        for part in range(3):
            tile, dp, at = along(orders[part][0], o)
            n = part * 3 + o - 1
            s1_send[n] = step1_part(part, at).reshape(128, PART).astype(BF16)
            copy = remote(s1_send.at[n], s1_recv.at[n], s1_ssem.at[n], s1_rsem.at[n], tile, dp)
            copy.start()
            copies.append(copy)
    for copy in copies:
        copy.wait()

    copies = []
    totals = []
    for part in range(3):
        total = step1_part(part, here[orders[part][0]])
        for o in range(3):
            total = total + s1_recv[part * 3 + o].astype(F32).reshape(16, 8, PART)
        s2_send[part] = total
    lead = (True, False, True)

    def step2_part(part, at):
        if lead[part]:
            return s2_send.at[part, pl.ds(at * 4, 4)]
        return s2_send.at[part, pl.ds(at, 4, stride=4)]

    for part in range(3):
        for o in (2, 1, 3):
            tile, dp, at = along(orders[part][1], o)
            n = part * 3 + o - 1
            if lead[part]:
                src = s2_send.at[part, pl.ds(at * 4, 4)]
            else:
                for i in range(4):
                    s3_send[n, i] = s2_send[part, i * 4 + at]
                src = s3_send.at[n]
            copy = remote(src, s2_recv.at[n], s2_ssem.at[n], s2_rsem.at[n], tile, dp)
            copy.start()
            copies.append(copy)
    for copy in copies:
        copy.wait()

    copies = []
    for part in range(3):
        at = here[orders[part][1]]
        if lead[part]:
            total = s2_send[part, pl.ds(at * 4, 4)]
        else:
            total = jnp.concatenate(
                [s2_send[part, pl.ds(i * 4 + at, 1)] for i in range(4)], axis=0
            )
        for o in range(3):
            total = total + s2_recv[part * 3 + o]
        fin_send[part] = total
        for o in (2, 1, 3):
            tile, dp, at = along(orders[part][2], o)
            n = part * 3 + o - 1
            copy = remote(
                fin_send.at[part, at], s3_recv.at[n], s3_ssem.at[n], s3_rsem.at[n], tile, dp
            )
            copy.start()
            copies.append(copy)
    for copy in copies:
        copy.wait()

    squares = jnp.zeros((8, C), F32)
    for part in range(3):
        total = fin_send[part, here[orders[part][2]]]
        for o in range(3):
            total = total + s3_recv[part * 3 + o]
        fin_recv[0, :, part * PART : (part + 1) * PART] = total
        for i in range(3):
            piece = total[:, i * C : (i + 1) * C]
            squares = squares + piece * piece
    fin_copy = remote(fin_recv.at[0], fin_recv.at[1], fin_sem.at[0], fin_sem.at[1], me_t, sib)
    fin_copy.start()

    nrm_send[...] = squares
    nrm_recv[0] = squares

    def n1_copy(o):
        return remote(nrm_send, nrm_recv.at[o], n1_ssem.at[o], n1_rsem.at[o], tile_peer(o), me_d)

    @pl.loop(1, N_TILE)
    def _(o):
        n1_copy(o).start()

    @pl.loop(1, N_TILE)
    def _(o):
        n1_copy(o).wait()

    plane = jnp.sum(nrm_recv[...], axis=0)
    nrm2_send[...] = plane
    nrm2_recv[me_d] = plane

    def n2_copy(o):
        return remote(
            nrm2_send, nrm2_recv.at[me_d], n2_ssem.at[o], n2_rsem.at[o], me_t, dp_peer(o)
        )

    @pl.loop(1, N_DP)
    def _(o):
        n2_copy(o).start()

    @pl.loop(1, N_DP)
    def _(o):
        n2_copy(o).wait()

    fin_copy.wait()
    total_a = jnp.sum(nrm2_recv[0] + nrm2_recv[2] + nrm2_recv[4] + nrm2_recv[6], keepdims=True)
    total_b = jnp.sum(nrm2_recv[1] + nrm2_recv[3] + nrm2_recv[5] + nrm2_recv[7], keepdims=True)
    root_a = jnp.sqrt(total_a / (HID * WIDE) + EPSILON)
    root_b = jnp.sqrt(total_b / (HID * WIDE) + EPSILON)
    first = core == 0
    full_a = jnp.where(first, fin_recv[0], fin_recv[1]) / root_a
    full_b = jnp.where(first, fin_recv[1], fin_recv[0]) / root_b
    upda_ref[...] = jnp.where(first, full_a[0:4], full_a[4:8])
    updb_ref[...] = jnp.where(first, full_b[0:4], full_b[4:8])


def local(*args):
    vmem = pl.BlockSpec(memory_space=pltpu.VMEM)
    smem = pl.BlockSpec(memory_space=pltpu.SMEM)
    hbm = pl.BlockSpec(memory_space=pl.ANY)
    dma = pltpu.SemaphoreType.DMA
    scratch = [
        pltpu.VMEM((64, 256, C), BF16),
        pltpu.VMEM((64, 256, C), F32),
        pltpu.VMEM((2, 64, C), F32),
        pltpu.VMEM((1, C), jnp.int32),
        pltpu.VMEM((N_TILE, 1, C), jnp.int32),
        pltpu.SMEM((N_TILE, 1, C), jnp.int32),
        pltpu.VMEM((N_TILE, 2, SIDE + 1, SIDE, C), BF16),
        pltpu.VMEM((N_TILE, 2, SIDE + 1, SIDE, C), BF16),
        pltpu.VMEM((NP, SIDE + 1, SIDE, C), BF16),
        pltpu.VMEM((NP, SIDE, C), F32),
        pltpu.VMEM((WIDE + C, HID), BF16),
        pltpu.VMEM((C, HID), F32),
        pltpu.VMEM((HID, WIDE), BF16),
        pltpu.VMEM((NP * SIDE, SIDE, WIDE + C), BF16),
        pltpu.VMEM((NP * SIDE, SIDE, WIDE), BF16),
        pltpu.VMEM((NP * CELLS, HID), BF16),
        pltpu.VMEM((NP * CELLS, HID), F32),
        pltpu.VMEM((NP * CELLS, HID), BF16),
        pltpu.VMEM((HID, WIDE), F32),
        pltpu.VMEM((HID, WIDE), F32),
        pltpu.VMEM((HID, WIDE), F32),
        pltpu.VMEM((9, 128, PART), BF16),
        pltpu.VMEM((9, 128, PART), BF16),
        pltpu.VMEM((3, 16, 8, PART), F32),
        pltpu.VMEM((9, 4, 8, PART), F32),
        pltpu.VMEM((9, 4, 8, PART), F32),
        pltpu.VMEM((9, 8, PART), F32),
        pltpu.VMEM((3, 4, 8, PART), F32),
        pltpu.VMEM((2, 8, WIDE), F32),
        pltpu.VMEM((8, C), F32),
        pltpu.VMEM((N_TILE, 8, C), F32),
        pltpu.VMEM((8, C), F32),
        pltpu.VMEM((N_DP, 8, C), F32),
        dma((3 + TAPS,)),
        dma((N_TILE,)),
        dma((N_TILE,)),
        dma((N_TILE,)),
        dma((N_TILE,)),
        dma((2,)),
        dma((9,)),
        dma((9,)),
        dma((9,)),
        dma((9,)),
        dma((9,)),
        dma((9,)),
        dma((2,)),
        dma((N_TILE,)),
        dma((N_TILE,)),
        dma((N_DP,)),
        dma((N_DP,)),
    ]
    return pl.pallas_call(
        kernel,
        out_shape=(
            jax.ShapeDtypeStruct((NP,), F32),
            jax.ShapeDtypeStruct((4, WIDE), F32),
            jax.ShapeDtypeStruct((4, WIDE), F32),
        ),
        in_specs=[hbm, vmem, smem, smem, smem, smem, smem, vmem, hbm, vmem, vmem, vmem, hbm, vmem, vmem],
        out_specs=(smem, vmem, vmem),
        scratch_shapes=scratch,
        compiler_params=pltpu.CompilerParams(
            collective_id=0, has_side_effects=True, vmem_limit_bytes=56 * 2**20
        ),
    )(*args)


def solution(mesh):
    both = ("tile", "dp")
    return jax.shard_map(
        local,
        mesh=mesh,
        in_specs=(
            P("tile", None, None),
            P("tile", None),
            P(both, None),
            P(both),
            P(both),
            P(both),
            P(both),
            P(both, None, None),
            P(),
            P(),
            P(),
            P(),
            P(),
            P(),
            P(),
        ),
        out_specs=(P(both), P(both, None), P(both, None)),
        check_vma=False,
    )
```

```python
import functools
import math

import jax
import jax.numpy as jnp
from jax import lax
from jax.experimental import pallas as pl
from jax.experimental.pallas import tpu as pltpu
from jax.sharding import PartitionSpec as P

C = 128
HID = 512
SIDE = 16
LEVELS = 32
NP = 4
CELLS = SIDE * SIDE
TAPS = 9
WIDE = TAPS * C
SIGMA_LOW = 0.02
SIGMA_HIGH = 80.0
SIGMA_DATA = 0.5
EPSILON = 1e-06
LOG_LOW = math.log(SIGMA_LOW)
LOG_STEP = (math.log(SIGMA_HIGH) - math.log(SIGMA_LOW)) / (LEVELS - 1)

MESH = pl.DeviceIdType.MESH
F32 = jnp.float32
BF16 = jnp.bfloat16
N_TILE = 16
N_DP = 8
AX = 4
PART = WIDE // 3


def iota(shape, dim):
    return lax.broadcasted_iota(jnp.int32, shape, dim)


def remote(src, dst, send_sem, recv_sem, tile, dp):
    return pltpu.make_async_remote_copy(
        src_ref=src,
        dst_ref=dst,
        send_sem=send_sem,
        recv_sem=recv_sem,
        device_id=(tile, dp),
        device_id_type=MESH,
    )


def column_shifts(block):
    col = iota(block.shape, 1)
    before = jnp.where(col == 0, 0.0, pltpu.roll(block, 1, axis=1))
    after = jnp.where(col == SIDE - 1, 0.0, pltpu.roll(block, SIDE - 1, axis=1))
    return before, block, after


def store_rows(dst, p, lane, rows, delta):
    lanes = slice(lane, lane + C)
    base = p * SIDE
    zero = jnp.zeros((1, SIDE, C), BF16)
    if delta == 0:
        dst[base : base + SIDE, :, lanes] = rows
    elif delta < 0:
        dst[base : base + 1, :, lanes] = zero
        dst[base + 1 : base + SIDE, :, lanes] = rows[: SIDE - 1]
    else:
        dst[base : base + SIDE - 1, :, lanes] = rows[1:]
        dst[base + SIDE - 1 : base + SIDE, :, lanes] = zero


def kernel(
    feat_hbm,
    tgt_hbm,
    owner_hbm,
    row_hbm,
    col_hbm,
    level_hbm,
    count_hbm,
    noise_hbm,
    wa_hbm,
    wu_hbm,
    ba_hbm,
    ea_hbm,
    wb_hbm,
    bb_hbm,
    wo_hbm,
    losses_ref,
    upda_ref,
    updb_ref,
    owner_ref,
    row_ref,
    col_ref,
    level_ref,
    count_ref,
    feat_v,
    feat_f,
    tgt_b,
    tgt_v,
    noise_b,
    noise_v,
    wu_ref,
    ba_ref,
    ea_ref,
    bb_ref,
    wo_ref,
    req_send,
    req_recv,
    req_smem,
    m1_send,
    m1_recv,
    m2_send,
    m2_recv0,
    m2_recv1,
    m2_recv2,
    m2_recv3,
    blk,
    wfull,
    wext,
    w2,
    left,
    right,
    slope,
    mine,
    sib_send,
    sib_recv,
    s1_send,
    s1_recv,
    tot2,
    s2_send,
    s2_recv,
    tot3,
    s3_recv,
    fin,
    nrm_send,
    nrm_recv,
    nrm2_send,
    nrm2_recv,
    local_sem,
    req_ssem,
    req_rsem,
    m1_ssem,
    m1_rsem,
    m2_ssem,
    m2_rsem,
    sib_ssem,
    sib_rsem,
    s1_ssem,
    s1_rsem,
    s2_ssem,
    s2_rsem,
    s3_ssem,
    s3_rsem,
    fin_sem,
    n1_ssem,
    n1_rsem,
    n2_ssem,
    n2_rsem,
):
    me_t = lax.axis_index("tile")
    me_d = lax.axis_index("dp")
    x, z = me_t >> 2, me_t & 3
    y, core = me_d >> 1, me_d & 1

    def tile_at(dx, dz):
        return (((x + dx) & 3) << 2) | ((z + dz) & 3)

    def tile_peer(o):
        return tile_at(o >> 2, o & 3)

    def dp_peer(o):
        return (me_d + o) & (N_DP - 1)

    m2_recv = (m2_recv0, m2_recv1, m2_recv2, m2_recv3)

    barrier = pltpu.get_barrier_semaphore()
    for o in range(1, N_TILE):
        pl.semaphore_signal(barrier, inc=1, device_id=(tile_peer(o), me_d), device_id_type=MESH)
    for o in range(1, N_DP):
        pl.semaphore_signal(barrier, inc=1, device_id=(me_t, dp_peer(o)), device_id_type=MESH)

    staged = []

    def stage(src, dst):
        copy = pltpu.make_async_copy(src, dst, local_sem.at[len(staged)])
        copy.start()
        staged.append(copy)
        return copy

    ints = [
        stage(a, b)
        for a, b in (
            (owner_hbm, owner_ref),
            (row_hbm, row_ref),
            (col_hbm, col_ref),
            (level_hbm, level_ref),
            (count_hbm, count_ref),
        )
    ]
    feat_copy = stage(feat_hbm, feat_v)
    tgt_copy = stage(tgt_hbm, tgt_b)
    small = [
        stage(a, b)
        for a, b in (
            (noise_hbm, noise_b),
            (wu_hbm, wu_ref),
            (ba_hbm, ba_ref),
            (ea_hbm, ea_ref),
            (bb_hbm, bb_ref),
            (wo_hbm, wo_ref),
        )
    ]
    small.append(stage(wa_hbm, wfull.at[pl.ds(0, WIDE)]))
    for t in range(TAPS):
        small.append(stage(wb_hbm.at[pl.ds(t * HID, HID)], w2.at[:, pl.ds(t * C, C)]))
    for copy in ints:
        copy.wait()

    lane = iota((1, C), 1)
    line = jnp.zeros((1, C), jnp.int32)
    for k in range(NP):
        line = jnp.where(lane == 4 * k, owner_ref[k], line)
        line = jnp.where(lane == 4 * k + 1, row_ref[k], line)
        line = jnp.where(lane == 4 * k + 2, col_ref[k], line)
    req_send[...] = line
    req_recv[me_t] = line
    pl.semaphore_wait(barrier, N_TILE - 1 + N_DP - 1)

    copies = []
    for o in range(1, N_TILE):
        copy = remote(
            req_send, req_recv.at[me_t], req_ssem.at[o], req_rsem.at[o], tile_peer(o), me_d
        )
        copy.start()
        copies.append(copy)

    tgt_copy.wait()
    tgt_v[0] = tgt_b[:, :C].astype(F32)
    tgt_v[1] = tgt_b[:, C:].astype(F32)
    feat_copy.wait()

    @pl.loop(0, 32)
    def _(i):
        feat_f[2 * i] = feat_v[2 * i].astype(F32)
        feat_f[2 * i + 1] = feat_v[2 * i + 1].astype(F32)

    for copy in copies:
        copy.wait()
    to_smem = pltpu.make_async_copy(req_recv, req_smem, local_sem.at[len(staged)])
    to_smem.start()
    to_smem.wait()

    lane2 = iota((SIDE, C), 1)

    def turn(value, shift):
        amount = jnp.full(value.shape, shift & (C - 1), jnp.int32)
        for bit in (1, 2, 4, 8, 16, 32, 64):
            value = jnp.where((amount & bit) != 0, pltpu.roll(value, bit, axis=1), value)
        return value

    def wanted(j):
        rank = jnp.int32(0)
        rows = [jnp.int32(0), jnp.int32(0)]
        cols = [jnp.int32(0), jnp.int32(0)]
        for k in range(NP):
            hit = req_smem[j, 0, 4 * k] == me_t
            for q in range(2):
                take = hit & (rank == q)
                rows[q] = jnp.where(take, req_smem[j, 0, 4 * k + 1], rows[q])
                cols[q] = jnp.where(take, req_smem[j, 0, 4 * k + 2], cols[q])
            rank = rank + hit.astype(jnp.int32)
        return rows, cols

    def fill(half, o, dst):
        def one(e, tile):
            rows, cols = wanted(tile_at(e, o) if half == 0 else tile_at(o, e))
            for q in range(2):
                block = feat_f[pl.ds(rows[q] + 8 * half, 8), pl.ds(cols[q], SIDE), :]
                dst[pl.ds((2 * e + q) * 8, 8)] = block.astype(BF16)
                if half == 0:
                    high = cols[q] >> 7
                    shift = cols[q] & (C - 1)
                    low_part = tgt_v[high, pl.ds(rows[q], SIDE), :]
                    next_part = tgt_v[1, pl.ds(rows[q], SIDE), :]
                    both = jnp.where(lane2 < shift, next_part, low_part)
                    both = turn(both, (2 * e + q) * SIDE - shift)
                    tile = jnp.where((lane2 >> 4) == 2 * e + q, both, tile)
            return tile

        tile = lax.fori_loop(0, AX, one, jnp.zeros((SIDE, C), F32))
        if half == 0:
            dst[64] = tile.astype(BF16)

    m1_copies = ([], [])
    for o in (2, 1, 3):
        for half in range(2):
            n = 3 * half + o - 1
            fill(half, o, m1_send.at[n])
            units = 65 - half
            copy = remote(
                m1_send.at[n, pl.ds(0, units)],
                m1_recv.at[half, o, pl.ds(0, units)],
                m1_ssem.at[n],
                m1_rsem.at[n],
                tile_at(0, o) if half == 0 else tile_at(o, 0),
                me_d,
            )
            copy.start()
            m1_copies[half].append(copy)
    for half in range(2):
        fill(half, 0, m1_recv.at[half, 0])

    for copy in small:
        copy.wait()
    wu = wu_ref[...]
    wu_hi = wu.astype(BF16).astype(F32)
    ba = ba_ref[...].reshape(1, HID)
    ba_hi = ba.astype(BF16).astype(F32)
    ea = ea_ref[...].reshape(1, HID)
    ea_hi = ea.astype(BF16).astype(F32)
    wext[...] = jnp.zeros_like(wext)
    wext[0:9] = wu_hi
    wext[9:18] = wu - wu_hi
    wext[18:27] = wu_hi
    wext[27:28] = ba_hi
    wext[28:29] = ba - ba_hi
    wext[29:30] = ea_hi
    wext[30:31] = ea - ea_hi
    wext[31:32] = ea_hi
    wfull[WIDE:, :] = wext[...].astype(BF16)
    noise_v[...] = jnp.zeros_like(noise_v)
    noise_v[:, :, 0:SIDE] = noise_b[...]

    for half in range(2):
        for copy in m1_copies[half]:
            copy.wait()

    def rank_of(j, k):
        rank = jnp.int32(0)
        for before in range(k):
            same = req_smem[j, 0, 4 * before] == req_smem[j, 0, 4 * k]
            rank = rank + same.astype(jnp.int32)
        return jnp.minimum(rank, 1)

    m2_copies = []
    for k in range(NP):
        row = []
        for e in (2, 1, 3, 0):
            for half in range(2):
                j = tile_at(e, 0) if half == 0 else tile_at(0, e)
                owner = req_smem[j, 0, 4 * k]
                rank = rank_of(j, k)
                if half == 0:
                    o = (z - (owner & 3)) & 3
                else:
                    o = (x - (owner >> 2)) & 3
                if e:
                    dst = m2_send.at[half * 4 + e, k]
                else:
                    dst = m2_recv[k].at[half, 0]
                dst[0:8] = m1_recv[half, o, pl.ds((2 * e + rank) * 8, 8)]
                if half == 0:
                    tile = m1_recv[0, o, 64].astype(F32)
                    if e:
                        tile = pltpu.roll(tile, C - 2 * e * SIDE, axis=1)
                    second = jnp.full(tile.shape, rank, jnp.int32) != 0
                    tile = jnp.where(second, pltpu.roll(tile, C - SIDE, axis=1), tile)
                    dst[8] = tile.astype(BF16)
                if e:
                    units = 9 - half
                    n = half * 16 + e * 4 + k
                    copy = remote(
                        m2_send.at[half * 4 + e, k, pl.ds(0, units)],
                        m2_recv[k].at[half, e, pl.ds(0, units)],
                        m2_ssem.at[n],
                        m2_rsem.at[n],
                        j,
                        me_d,
                    )
                    copy.start()
                    row.append(copy)
        m2_copies.append(row)

    wo = wo_ref[...].reshape(1, 1, C)
    bb = bb_ref[...].reshape(1, 1, C)
    shape3 = (SIDE, SIDE, C)
    col3, lane3 = iota(shape3, 1), iota(shape3, 2)
    none = jnp.zeros((1, SIDE, C), F32)
    for p in range(NP):
        for copy in m2_copies[p]:
            copy.wait()
        owner = owner_ref[p]
        from_x, from_z = (x - (owner >> 2)) & 3, (z - (owner & 3)) & 3
        blk[0:8] = m2_recv[p][0, from_x, 0:8]
        blk[8:16] = m2_recv[p][1, from_z, 0:8]
        clean = jnp.where(lane2 < SIDE, m2_recv[p][0, from_x, 8].astype(F32), 0.0)
        xcol = right.at[0]
        gcol = right.at[1]
        block = blk[...].astype(F32)
        for s, moved in enumerate(column_shifts(block)):
            rows = moved.astype(BF16)
            for r in range(3):
                store_rows(xcol, p, (3 * r + s) * C, rows, r - 1)

        level = jnp.full((SIDE, C), level_ref[p], jnp.int32).astype(F32)
        sigma = jnp.exp(LOG_LOW + level * LOG_STEP)
        variance = sigma * sigma + SIGMA_DATA * SIGMA_DATA
        scale_in = 1.0 / jnp.sqrt(variance)
        scale_skip = SIGMA_DATA * SIGMA_DATA / variance
        scale_out = sigma * SIGMA_DATA * scale_in
        embed = jnp.log(sigma) / 4.0
        noisy = clean + sigma * noise_v[p]
        aim = (clean - scale_skip * noisy) / scale_out
        scaled = pltpu.roll(scale_in * noisy, 1, axis=1)
        wide = jnp.broadcast_to(scaled[:, None, :], shape3)
        for bit in (1, 2, 4, 8):
            wide = jnp.where((col3 & bit) != 0, pltpu.roll(wide, C - bit, axis=2), wide)
        wide = jnp.where(lane3 < 3, wide, 0.0)
        taps = (
            jnp.concatenate([none, wide[: SIDE - 1]], axis=0)
            + pltpu.roll(wide, 3, axis=2)
            + pltpu.roll(jnp.concatenate([wide[1:], none], axis=0), 6, axis=2)
        )
        taps_hi = taps.astype(BF16).astype(F32)
        emb = embed[0:1, :][None]
        emb_hi = emb.astype(BF16).astype(F32)
        extra = taps_hi + pltpu.roll(taps_hi, 9, axis=2) + pltpu.roll(taps - taps_hi, 18, axis=2)
        extra = jnp.where((lane3 == 27) | (lane3 == 28), 1.0, extra)
        extra = jnp.where((lane3 == 29) | (lane3 == 30), emb_hi, extra)
        extra = jnp.where(lane3 == 31, emb - emb_hi, extra)
        xcol[p * SIDE : (p + 1) * SIDE, :, WIDE:] = extra.astype(BF16)

        cells = slice(p * CELLS, (p + 1) * CELLS)
        window = xcol[p * SIDE : (p + 1) * SIDE].reshape(CELLS, WIDE + C)
        pre_a = jnp.dot(window, wfull[...], preferred_element_type=F32)
        gate = jax.nn.sigmoid(pre_a)
        slope[...] = gate * (1.0 + pre_a * (1.0 - gate))
        hidden = (pre_a * gate).astype(BF16)
        left[1, cells] = hidden

        spread = jnp.dot(hidden, w2[...], preferred_element_type=F32).reshape(SIDE, SIDE, WIDE)

        def tap_rows(s):
            up = spread[:, :, s * C : (s + 1) * C]
            mid = spread[:, :, (3 + s) * C : (4 + s) * C]
            down = spread[:, :, (6 + s) * C : (7 + s) * C]
            return (
                mid
                + jnp.concatenate([none, up[: SIDE - 1]], axis=0)
                + jnp.concatenate([down[1:], none], axis=0)
            )

        before = jnp.where(col3 == 0, 0.0, pltpu.roll(tap_rows(0), 1, axis=1))
        after = jnp.where(col3 == SIDE - 1, 0.0, pltpu.roll(tap_rows(2), SIDE - 1, axis=1))
        pre_b = bb + tap_rows(1) + before + after
        gate_b = jax.nn.sigmoid(pre_b)
        aim3 = jnp.where(col3 == lane3, jnp.broadcast_to(aim[:, None, :], shape3), 0.0)
        residual = jnp.sum(pre_b * gate_b * wo - aim3, axis=2, keepdims=True)
        weight = count_ref[p].astype(F32)
        losses_ref[p] = jnp.sum(residual * residual) * weight / CELLS
        grad_final = (2.0 * weight / CELLS) * residual
        grad_b = grad_final * wo * (gate_b * (1.0 + pre_b * (1.0 - gate_b)))
        grad_b = grad_b.astype(BF16).astype(F32)
        for s, moved in enumerate(column_shifts(grad_b)):
            rows = moved.astype(BF16)
            for r in range(3):
                store_rows(gcol, p, (3 * (2 - r) + (2 - s)) * C, rows, r - 1)

        back = lax.dot_general(
            gcol[p * SIDE : (p + 1) * SIDE, :, 0:WIDE].reshape(CELLS, WIDE),
            w2[...],
            (((1,), (1,)), ((), ())),
            preferred_element_type=F32,
        )
        left[0, cells] = (back * slope[...]).astype(BF16)

    sib = me_d ^ 1

    def gradient(which, part):
        return lax.dot_general(
            left[which],
            right[which, :, :, part * PART : (part + 1) * PART].reshape(NP * CELLS, PART),
            (((0,), (0,)), ((), ())),
            preferred_element_type=F32,
        )

    def along(axis, o):
        if axis == 0:
            at = (x + o) & 3
            return (at << 2) | z, me_d, at
        if axis == 1:
            at = (z + o) & 3
            return (x << 2) | at, me_d, at
        at = (y + o) & 3
        return me_t, (at << 1) | core, at

    here = (x, z, y)
    orders = ((0, 1, 2), (1, 2, 0), (2, 0, 1))
    full = (AX, AX, 8, PART)

    def piece1(part, at):
        if part == 0:
            return mine[part, at]
        if part == 1:
            return mine[part, :, at]
        return mine[part, :, :, at]

    s1_copies = []

    def step1(part):
        sib_copies[part].wait()
        mine[part] = mine[part] + sib_recv[part].astype(F32).reshape(AX, AX, AX, 8, PART)
        row = []
        for o in (2, 1, 3):
            tile, dp, at = along(orders[part][0], o)
            n = part * 3 + o - 1
            s1_send[n] = piece1(part, at).reshape(128, PART).astype(BF16)
            copy = remote(s1_send.at[n], s1_recv.at[n], s1_ssem.at[n], s1_rsem.at[n], tile, dp)
            copy.start()
            row.append(copy)
        s1_copies.append(row)

    sib_copies = []
    for part in range(3):
        sib_send[part] = gradient(1 - core, part).astype(BF16)
        copy = remote(
            sib_send.at[part], sib_recv.at[part], sib_ssem.at[part], sib_rsem.at[part], me_t, sib
        )
        copy.start()
        sib_copies.append(copy)
        mine[part] = gradient(core, part).reshape(AX, AX, AX, 8, PART)
        if part:
            step1(part - 1)
    step1(2)

    def piece2(part, at):
        return tot2[part, :, at] if part == 1 else tot2[part, at]

    s2_copies = []
    for part in range(3):
        for copy in s1_copies[part]:
            copy.wait()
        total = piece1(part, here[orders[part][0]])
        for o in range(3):
            total = total + s1_recv[part * 3 + o].astype(F32).reshape(full)
        tot2[part] = total
        row = []
        for o in (2, 1, 3):
            tile, dp, at = along(orders[part][1], o)
            n = part * 3 + o - 1
            s2_send[n] = piece2(part, at).reshape(32, PART).astype(BF16)
            copy = remote(s2_send.at[n], s2_recv.at[n], s2_ssem.at[n], s2_rsem.at[n], tile, dp)
            copy.start()
            row.append(copy)
        s2_copies.append(row)

    s3_copies = []
    for part in range(3):
        for copy in s2_copies[part]:
            copy.wait()
        total = piece2(part, here[orders[part][1]])
        for o in range(3):
            total = total + s2_recv[part * 3 + o].astype(F32).reshape(AX, 8, PART)
        tot3[part] = total
        row = []
        for o in (2, 1, 3):
            tile, dp, at = along(orders[part][2], o)
            n = part * 3 + o - 1
            copy = remote(
                tot3.at[part, at], s3_recv.at[n], s3_ssem.at[n], s3_rsem.at[n], tile, dp
            )
            copy.start()
            row.append(copy)
        s3_copies.append(row)

    squares = jnp.zeros((8, C), F32)
    for part in range(3):
        for copy in s3_copies[part]:
            copy.wait()
        total = tot3[part, here[orders[part][2]]]
        for o in range(3):
            total = total + s3_recv[part * 3 + o]
        fin[0, :, part * PART : (part + 1) * PART] = total
        for i in range(3):
            piece = total[:, i * C : (i + 1) * C]
            squares = squares + piece * piece

    nrm_send[...] = squares
    nrm_recv[0] = squares
    copies = []
    for o in range(1, N_TILE):
        copy = remote(nrm_send, nrm_recv.at[o], n1_ssem.at[o], n1_rsem.at[o], tile_peer(o), me_d)
        copy.start()
        copies.append(copy)
    fin_copy = remote(fin.at[0], fin.at[1], fin_sem.at[0], fin_sem.at[1], me_t, sib)
    fin_copy.start()
    for copy in copies:
        copy.wait()
    plane = jnp.sum(nrm_recv[...], axis=0)
    nrm2_send[...] = plane
    nrm2_recv[me_d] = plane
    copies = []
    for o in range(1, N_DP):
        copy = remote(
            nrm2_send, nrm2_recv.at[me_d], n2_ssem.at[o], n2_rsem.at[o], me_t, dp_peer(o)
        )
        copy.start()
        copies.append(copy)
    fin_copy.wait()
    for copy in copies:
        copy.wait()

    total_a = jnp.sum(nrm2_recv[0] + nrm2_recv[2] + nrm2_recv[4] + nrm2_recv[6], keepdims=True)
    total_b = jnp.sum(nrm2_recv[1] + nrm2_recv[3] + nrm2_recv[5] + nrm2_recv[7], keepdims=True)
    root_a = jnp.sqrt(total_a / (HID * WIDE) + EPSILON)
    root_b = jnp.sqrt(total_b / (HID * WIDE) + EPSILON)
    full_a = fin[core] / root_a
    full_b = fin[1 - core] / root_b
    first = core == 0
    upda_ref[...] = jnp.where(first, full_a[0:4], full_a[4:8])
    updb_ref[...] = jnp.where(first, full_b[0:4], full_b[4:8])


def leave(a_in, b_in, c_in, a_out, b_out, c_out, sem):
    pairs = ((a_in, a_out), (b_in, b_out), (c_in, c_out))
    copies = [pltpu.make_async_copy(s, d, sem.at[i]) for i, (s, d) in enumerate(pairs)]
    for copy in copies:
        copy.start()
    for copy in copies:
        copy.wait()


def local(features, target_field, owner_tile, *rest):
    vmem = pl.BlockSpec(memory_space=pltpu.VMEM)
    smem = pl.BlockSpec(memory_space=pltpu.SMEM)
    hbm = pl.BlockSpec(memory_space=pl.ANY)
    dma = pltpu.SemaphoreType.DMA
    ints = pltpu.SMEM((NP,), jnp.int32)
    scratch = [
        ints,
        ints,
        ints,
        ints,
        ints,
        pltpu.VMEM((64, 256, C), BF16),
        pltpu.VMEM((64, 256, C), F32),
        pltpu.VMEM((64, 256), BF16),
        pltpu.VMEM((2, 64, C), F32),
        pltpu.VMEM((NP, SIDE, SIDE), F32),
        pltpu.VMEM((NP, SIDE, C), F32),
        pltpu.VMEM((TAPS, HID), F32),
        pltpu.VMEM((HID,), F32),
        pltpu.VMEM((HID,), F32),
        pltpu.VMEM((C,), F32),
        pltpu.VMEM((C,), F32),
        pltpu.VMEM((1, C), jnp.int32),
        pltpu.VMEM((N_TILE, 1, C), jnp.int32),
        pltpu.SMEM((N_TILE, 1, C), jnp.int32),
        pltpu.VMEM((6, 65, SIDE, C), BF16),
        pltpu.VMEM((2, AX, 65, SIDE, C), BF16),
        pltpu.VMEM((8, NP, 9, SIDE, C), BF16),
        pltpu.VMEM((2, AX, 9, SIDE, C), BF16),
        pltpu.VMEM((2, AX, 9, SIDE, C), BF16),
        pltpu.VMEM((2, AX, 9, SIDE, C), BF16),
        pltpu.VMEM((2, AX, 9, SIDE, C), BF16),
        pltpu.VMEM((SIDE, SIDE, C), BF16),
        pltpu.VMEM((WIDE + C, HID), BF16),
        pltpu.VMEM((C, HID), F32),
        pltpu.VMEM((HID, WIDE), BF16),
        pltpu.VMEM((2, NP * CELLS, HID), BF16),
        pltpu.VMEM((2, NP * SIDE, SIDE, WIDE + C), BF16),
        pltpu.VMEM((CELLS, HID), F32),
        pltpu.VMEM((3, AX, AX, AX, 8, PART), F32),
        pltpu.VMEM((3, HID, PART), BF16),
        pltpu.VMEM((3, HID, PART), BF16),
        pltpu.VMEM((9, 128, PART), BF16),
        pltpu.VMEM((9, 128, PART), BF16),
        pltpu.VMEM((3, AX, AX, 8, PART), F32),
        pltpu.VMEM((9, 32, PART), BF16),
        pltpu.VMEM((9, 32, PART), BF16),
        pltpu.VMEM((3, AX, 8, PART), F32),
        pltpu.VMEM((9, 8, PART), F32),
        pltpu.VMEM((2, 8, WIDE), F32),
        pltpu.VMEM((8, C), F32),
        pltpu.VMEM((N_TILE, 8, C), F32),
        pltpu.VMEM((8, C), F32),
        pltpu.VMEM((N_DP, 8, C), F32),
        dma((32,)),
        dma((N_TILE,)),
        dma((N_TILE,)),
        dma((6,)),
        dma((6,)),
        dma((32,)),
        dma((32,)),
        dma((3,)),
        dma((3,)),
        dma((9,)),
        dma((9,)),
        dma((9,)),
        dma((9,)),
        dma((9,)),
        dma((9,)),
        dma((2,)),
        dma((N_TILE,)),
        dma((N_TILE,)),
        dma((N_DP,)),
        dma((N_DP,)),
    ]
    outs = (
        jax.ShapeDtypeStruct((NP,), F32),
        jax.ShapeDtypeStruct((4, WIDE), F32),
        jax.ShapeDtypeStruct((4, WIDE), F32),
    )
    results = pl.pallas_call(
        kernel,
        out_shape=outs,
        in_specs=[hbm] * 15,
        out_specs=(smem, vmem, vmem),
        scratch_shapes=scratch,
        compiler_params=pltpu.CompilerParams(
            collective_id=0, has_side_effects=True, vmem_limit_bytes=60 * 2**20
        ),
    )(features, target_field, owner_tile.reshape(-1), *rest)
    return pl.pallas_call(
        leave,
        out_shape=outs,
        in_specs=[hbm] * 3,
        out_specs=(hbm,) * 3,
        scratch_shapes=[dma((3,))],
    )(*results)


def solution(mesh):
    both = ("tile", "dp")
    return jax.shard_map(
        local,
        mesh=mesh,
        in_specs=(
            P("tile", None, None),
            P("tile", None),
            P(both, None),
            P(both),
            P(both),
            P(both),
            P(both),
            P(both, None, None),
            P(),
            P(),
            P(),
            P(),
            P(),
            P(),
            P(),
        ),
        out_specs=(P(both), P(both, None), P(both, None)),
        check_vma=False,
    )
```

```python
import functools
import math

import jax
import jax.numpy as jnp
from jax import lax
from jax.experimental import pallas as pl
from jax.experimental.pallas import tpu as pltpu
from jax.sharding import PartitionSpec as P

C = 128
HID = 512
SIDE = 16
LEVELS = 32
NP = 4
CELLS = SIDE * SIDE
TAPS = 9
WIDE = TAPS * C
SIGMA_LOW = 0.02
SIGMA_HIGH = 80.0
SIGMA_DATA = 0.5
EPSILON = 1e-06
LOG_LOW = math.log(SIGMA_LOW)
LOG_STEP = (math.log(SIGMA_HIGH) - math.log(SIGMA_LOW)) / (LEVELS - 1)

MESH = pl.DeviceIdType.MESH
F32 = jnp.float32
BF16 = jnp.bfloat16
N_TILE = 16
N_DP = 8
AX = 4
PART = WIDE // 3


def iota(shape, dim):
    return lax.broadcasted_iota(jnp.int32, shape, dim)


def remote(src, dst, send_sem, recv_sem, tile, dp):
    return pltpu.make_async_remote_copy(
        src_ref=src,
        dst_ref=dst,
        send_sem=send_sem,
        recv_sem=recv_sem,
        device_id=(tile, dp),
        device_id_type=MESH,
    )


def column_shifts(block):
    col = iota(block.shape, 1)
    before = jnp.where(col == 0, 0.0, pltpu.roll(block, 1, axis=1))
    after = jnp.where(col == SIDE - 1, 0.0, pltpu.roll(block, SIDE - 1, axis=1))
    return before, block, after


def store_rows(dst, p, lane, rows, delta):
    lanes = slice(lane, lane + C)
    base = p * SIDE
    zero = jnp.zeros((1, SIDE, C), BF16)
    if delta == 0:
        dst[base : base + SIDE, :, lanes] = rows
    elif delta < 0:
        dst[base : base + 1, :, lanes] = zero
        dst[base + 1 : base + SIDE, :, lanes] = rows[: SIDE - 1]
    else:
        dst[base : base + SIDE - 1, :, lanes] = rows[1:]
        dst[base + SIDE - 1 : base + SIDE, :, lanes] = zero


def kernel(
    feat_hbm,
    tgt_hbm,
    owner_hbm,
    row_hbm,
    col_hbm,
    level_hbm,
    count_hbm,
    noise_hbm,
    wa_hbm,
    wu_hbm,
    ba_hbm,
    ea_hbm,
    wb_hbm,
    bb_hbm,
    wo_hbm,
    losses_ref,
    upda_ref,
    updb_ref,
    owner_ref,
    row_ref,
    col_ref,
    level_ref,
    count_ref,
    feat_v,
    feat_f,
    tgt_b,
    tgt_v,
    noise_b,
    noise_v,
    wu_ref,
    ba_ref,
    ea_ref,
    bb_ref,
    wo_ref,
    req_send,
    req_recv,
    req_smem,
    m1_send,
    m1_recv,
    m2_send,
    m2_recv0,
    m2_recv1,
    m2_recv2,
    m2_recv3,
    blk,
    wfull,
    wext,
    w2,
    left,
    right,
    slope,
    mine,
    s1_send,
    s1_recv,
    tot2,
    s2_send,
    s2_recv,
    tot3,
    s3_recv,
    fin,
    nrm_send,
    nrm_recv,
    nrm2_send,
    nrm2_recv,
    local_sem,
    req_ssem,
    req_rsem,
    m1_ssem,
    m1_rsem,
    m2_ssem,
    m2_rsem,
    sib_ssem,
    sib_rsem,
    s1_ssem,
    s1_rsem,
    s2_ssem,
    s2_rsem,
    s3_ssem,
    s3_rsem,
    fin_sem,
    n1_ssem,
    n1_rsem,
    n2_ssem,
    n2_rsem,
):
    me_t = lax.axis_index("tile")
    me_d = lax.axis_index("dp")
    x, z = me_t >> 2, me_t & 3
    y, core = me_d >> 1, me_d & 1

    def tile_at(dx, dz):
        return (((x + dx) & 3) << 2) | ((z + dz) & 3)

    def tile_peer(o):
        return tile_at(o >> 2, o & 3)

    def dp_peer(o):
        return (me_d + o) & (N_DP - 1)

    m2_recv = (m2_recv0, m2_recv1, m2_recv2, m2_recv3)

    barrier = pltpu.get_barrier_semaphore()
    staged = []

    def stage(src, dst):
        copy = pltpu.make_async_copy(src, dst, local_sem.at[len(staged)])
        copy.start()
        staged.append(copy)
        return copy

    ints = [
        stage(a, b)
        for a, b in (
            (owner_hbm, owner_ref),
            (row_hbm, row_ref),
            (col_hbm, col_ref),
            (level_hbm, level_ref),
            (count_hbm, count_ref),
        )
    ]
    for o in range(1, N_TILE):
        pl.semaphore_signal(barrier, inc=1, device_id=(tile_peer(o), me_d), device_id_type=MESH)
    for o in range(1, N_DP):
        pl.semaphore_signal(barrier, inc=1, device_id=(me_t, dp_peer(o)), device_id_type=MESH)

    feat_copy = stage(feat_hbm, feat_v)
    tgt_copy = stage(tgt_hbm, tgt_b)
    small = [
        stage(a, b)
        for a, b in (
            (noise_hbm, noise_b),
            (wu_hbm, wu_ref),
            (ba_hbm, ba_ref),
            (ea_hbm, ea_ref),
            (bb_hbm, bb_ref),
            (wo_hbm, wo_ref),
        )
    ]
    small.append(stage(wa_hbm, wfull.at[pl.ds(0, WIDE)]))
    for t in range(TAPS):
        small.append(stage(wb_hbm.at[pl.ds(t * HID, HID)], w2.at[:, pl.ds(t * C, C)]))
    for copy in ints:
        copy.wait()

    lane = iota((1, C), 1)
    line = jnp.zeros((1, C), jnp.int32)
    for k in range(NP):
        line = jnp.where(lane == 4 * k, owner_ref[k], line)
        line = jnp.where(lane == 4 * k + 1, row_ref[k], line)
        line = jnp.where(lane == 4 * k + 2, col_ref[k], line)
    req_send[...] = line
    req_recv[me_t] = line
    pl.semaphore_wait(barrier, N_TILE - 1 + N_DP - 1)

    copies = []
    for o in range(1, N_TILE):
        copy = remote(
            req_send, req_recv.at[me_t], req_ssem.at[o], req_rsem.at[o], tile_peer(o), me_d
        )
        copy.start()
        copies.append(copy)

    tgt_copy.wait()
    tgt_v[0] = tgt_b[:, :C].astype(F32)
    tgt_v[1] = tgt_b[:, C:].astype(F32)
    feat_copy.wait()

    @pl.loop(0, 32)
    def _(i):
        feat_f[2 * i] = feat_v[2 * i].astype(F32)
        feat_f[2 * i + 1] = feat_v[2 * i + 1].astype(F32)

    for copy in copies:
        copy.wait()
    to_smem = pltpu.make_async_copy(req_recv, req_smem, local_sem.at[len(staged)])
    to_smem.start()
    to_smem.wait()

    lane2 = iota((SIDE, C), 1)

    def turn(value, shift):
        amount = jnp.full(value.shape, shift & (C - 1), jnp.int32)
        for bit in (1, 2, 4, 8, 16, 32, 64):
            value = jnp.where((amount & bit) != 0, pltpu.roll(value, bit, axis=1), value)
        return value

    def wanted(j):
        rank = jnp.int32(0)
        rows = [jnp.int32(0), jnp.int32(0)]
        cols = [jnp.int32(0), jnp.int32(0)]
        for k in range(NP):
            hit = req_smem[j, 0, 4 * k] == me_t
            for q in range(2):
                take = hit & (rank == q)
                rows[q] = jnp.where(take, req_smem[j, 0, 4 * k + 1], rows[q])
                cols[q] = jnp.where(take, req_smem[j, 0, 4 * k + 2], cols[q])
            rank = rank + hit.astype(jnp.int32)
        return rows, cols

    def fill(half, o, dst):
        def one(e, tile):
            rows, cols = wanted(tile_at(e, o) if half == 0 else tile_at(o, e))
            for q in range(2):
                block = feat_f[pl.ds(rows[q] + 8 * half, 8), pl.ds(cols[q], SIDE), :]
                dst[pl.ds((2 * e + q) * 8, 8)] = block.astype(BF16)
                if half == 0:
                    high = cols[q] >> 7
                    shift = cols[q] & (C - 1)
                    low_part = tgt_v[high, pl.ds(rows[q], SIDE), :]
                    next_part = tgt_v[1, pl.ds(rows[q], SIDE), :]
                    both = jnp.where(lane2 < shift, next_part, low_part)
                    both = turn(both, (2 * e + q) * SIDE - shift)
                    tile = jnp.where((lane2 >> 4) == 2 * e + q, both, tile)
            return tile

        tile = lax.fori_loop(0, AX, one, jnp.zeros((SIDE, C), F32), unroll=True)
        if half == 0:
            dst[64] = tile.astype(BF16)

    m1_copies = ([], [])
    for o in (2, 1, 3):
        for half in range(2):
            n = 3 * half + o - 1
            fill(half, o, m1_send.at[n])
            units = 65 - half
            copy = remote(
                m1_send.at[n, pl.ds(0, units)],
                m1_recv.at[half, o, pl.ds(0, units)],
                m1_ssem.at[n],
                m1_rsem.at[n],
                tile_at(0, o) if half == 0 else tile_at(o, 0),
                me_d,
            )
            copy.start()
            m1_copies[half].append(copy)
    for half in range(2):
        fill(half, 0, m1_recv.at[half, 0])

    for copy in small:
        copy.wait()
    wu = wu_ref[...]
    wu_hi = wu.astype(BF16).astype(F32)
    ba = ba_ref[...].reshape(1, HID)
    ba_hi = ba.astype(BF16).astype(F32)
    ea = ea_ref[...].reshape(1, HID)
    ea_hi = ea.astype(BF16).astype(F32)
    wext[...] = jnp.zeros_like(wext)
    wext[0:9] = wu_hi
    wext[9:18] = wu - wu_hi
    wext[18:27] = wu_hi
    wext[27:28] = ba_hi
    wext[28:29] = ba - ba_hi
    wext[29:30] = ea_hi
    wext[30:31] = ea - ea_hi
    wext[31:32] = ea_hi
    wfull[WIDE:, :] = wext[...].astype(BF16)
    noise_v[...] = jnp.zeros_like(noise_v)
    noise_v[:, :, 0:SIDE] = noise_b[...]

    for half in range(2):
        for copy in m1_copies[half]:
            copy.wait()

    def rank_of(j, k):
        rank = jnp.int32(0)
        for before in range(k):
            same = req_smem[j, 0, 4 * before] == req_smem[j, 0, 4 * k]
            rank = rank + same.astype(jnp.int32)
        return jnp.minimum(rank, 1)

    m2_copies = []
    for k in range(NP):
        row = []
        for e in (2, 1, 3, 0):
            for half in range(2):
                j = tile_at(e, 0) if half == 0 else tile_at(0, e)
                owner = req_smem[j, 0, 4 * k]
                rank = rank_of(j, k)
                if half == 0:
                    o = (z - (owner & 3)) & 3
                else:
                    o = (x - (owner >> 2)) & 3
                if e:
                    dst = m2_send.at[half * 4 + e, k]
                else:
                    dst = m2_recv[k].at[half, 0]
                dst[0:8] = m1_recv[half, o, pl.ds((2 * e + rank) * 8, 8)]
                if half == 0:
                    tile = m1_recv[0, o, 64].astype(F32)
                    if e:
                        tile = pltpu.roll(tile, C - 2 * e * SIDE, axis=1)
                    second = jnp.full(tile.shape, rank, jnp.int32) != 0
                    tile = jnp.where(second, pltpu.roll(tile, C - SIDE, axis=1), tile)
                    dst[8] = tile.astype(BF16)
                if e:
                    units = 9 - half
                    n = half * 16 + e * 4 + k
                    copy = remote(
                        m2_send.at[half * 4 + e, k, pl.ds(0, units)],
                        m2_recv[k].at[half, e, pl.ds(0, units)],
                        m2_ssem.at[n],
                        m2_rsem.at[n],
                        j,
                        me_d,
                    )
                    copy.start()
                    row.append(copy)
        m2_copies.append(row)

    sib = me_d ^ 1
    pair_copies = []
    wo = wo_ref[...].reshape(1, 1, C)
    bb = bb_ref[...].reshape(1, 1, C)
    shape3 = (SIDE, SIDE, C)
    col3, lane3 = iota(shape3, 1), iota(shape3, 2)
    none = jnp.zeros((1, SIDE, C), F32)
    for p in range(NP):
        for copy in m2_copies[p]:
            copy.wait()
        owner = owner_ref[p]
        from_x, from_z = (x - (owner >> 2)) & 3, (z - (owner & 3)) & 3
        blk[0:8] = m2_recv[p][0, from_x, 0:8]
        blk[8:16] = m2_recv[p][1, from_z, 0:8]
        clean = jnp.where(lane2 < SIDE, m2_recv[p][0, from_x, 8].astype(F32), 0.0)
        xcol = right.at[0]
        gcol = right.at[1]
        block = blk[...].astype(F32)
        for s, moved in enumerate(column_shifts(block)):
            rows = moved.astype(BF16)
            for r in range(3):
                store_rows(xcol, p, (3 * r + s) * C, rows, r - 1)

        level = jnp.full((SIDE, C), level_ref[p], jnp.int32).astype(F32)
        sigma = jnp.exp(LOG_LOW + level * LOG_STEP)
        variance = sigma * sigma + SIGMA_DATA * SIGMA_DATA
        scale_in = 1.0 / jnp.sqrt(variance)
        scale_skip = SIGMA_DATA * SIGMA_DATA / variance
        scale_out = sigma * SIGMA_DATA * scale_in
        embed = jnp.log(sigma) / 4.0
        noisy = clean + sigma * noise_v[p]
        aim = (clean - scale_skip * noisy) / scale_out
        scaled = pltpu.roll(scale_in * noisy, 1, axis=1)
        wide = jnp.broadcast_to(scaled[:, None, :], shape3)
        for bit in (1, 2, 4, 8):
            wide = jnp.where((col3 & bit) != 0, pltpu.roll(wide, C - bit, axis=2), wide)
        wide = jnp.where(lane3 < 3, wide, 0.0)
        taps = (
            jnp.concatenate([none, wide[: SIDE - 1]], axis=0)
            + pltpu.roll(wide, 3, axis=2)
            + pltpu.roll(jnp.concatenate([wide[1:], none], axis=0), 6, axis=2)
        )
        taps_hi = taps.astype(BF16).astype(F32)
        emb = embed[0:1, :][None]
        emb_hi = emb.astype(BF16).astype(F32)
        extra = taps_hi + pltpu.roll(taps_hi, 9, axis=2) + pltpu.roll(taps - taps_hi, 18, axis=2)
        extra = jnp.where((lane3 == 27) | (lane3 == 28), 1.0, extra)
        extra = jnp.where((lane3 == 29) | (lane3 == 30), emb_hi, extra)
        extra = jnp.where(lane3 == 31, emb - emb_hi, extra)
        xcol[p * SIDE : (p + 1) * SIDE, :, WIDE:] = extra.astype(BF16)

        cells = slice(p * CELLS, (p + 1) * CELLS)
        window = xcol[p * SIDE : (p + 1) * SIDE].reshape(CELLS, WIDE + C)
        pre_a = jnp.dot(window, wfull[...], preferred_element_type=F32)
        gate = jax.nn.sigmoid(pre_a)
        slope[...] = gate * (1.0 + pre_a * (1.0 - gate))
        hidden = (pre_a * gate).astype(BF16)
        left[1, cells] = hidden

        spread = jnp.dot(hidden, w2[...], preferred_element_type=F32).reshape(SIDE, SIDE, WIDE)

        def tap_rows(s):
            up = spread[:, :, s * C : (s + 1) * C]
            mid = spread[:, :, (3 + s) * C : (4 + s) * C]
            down = spread[:, :, (6 + s) * C : (7 + s) * C]
            return (
                mid
                + jnp.concatenate([none, up[: SIDE - 1]], axis=0)
                + jnp.concatenate([down[1:], none], axis=0)
            )

        before = jnp.where(col3 == 0, 0.0, pltpu.roll(tap_rows(0), 1, axis=1))
        after = jnp.where(col3 == SIDE - 1, 0.0, pltpu.roll(tap_rows(2), SIDE - 1, axis=1))
        pre_b = bb + tap_rows(1) + before + after
        gate_b = jax.nn.sigmoid(pre_b)
        aim3 = jnp.where(col3 == lane3, jnp.broadcast_to(aim[:, None, :], shape3), 0.0)
        residual = jnp.sum(pre_b * gate_b * wo - aim3, axis=2, keepdims=True)
        weight = count_ref[p].astype(F32)
        losses_ref[p] = jnp.sum(residual * residual) * weight / CELLS
        grad_final = (2.0 * weight / CELLS) * residual
        grad_b = grad_final * wo * (gate_b * (1.0 + pre_b * (1.0 - gate_b)))
        grad_b = grad_b.astype(BF16).astype(F32)
        for s, moved in enumerate(column_shifts(grad_b)):
            rows = moved.astype(BF16)
            for r in range(3):
                store_rows(gcol, p, (3 * (2 - r) + (2 - s)) * C, rows, r - 1)

        back = lax.dot_general(
            gcol[p * SIDE : (p + 1) * SIDE, :, 0:WIDE].reshape(CELLS, WIDE),
            w2[...],
            (((1,), (1,)), ((), ())),
            preferred_element_type=F32,
        )
        left[0, cells] = (back * slope[...]).astype(BF16)

        row = []
        for i, ref in enumerate((left, right)):
            size = CELLS if i == 0 else SIDE
            lanes = pl.ds(0, HID if i == 0 else WIDE)
            middle = () if i == 0 else (slice(None),)
            copy = remote(
                ref.at[(1 - core, pl.ds(p * size, size)) + middle + (lanes,)],
                ref.at[(1 - core, pl.ds((NP + p) * size, size)) + middle + (lanes,)],
                sib_ssem.at[2 * p + i],
                sib_rsem.at[2 * p + i],
                me_t,
                sib,
            )
            copy.start()
            row.append(copy)
        pair_copies.append(row)

    for row in pair_copies[: NP - 1]:
        for copy in row:
            copy.wait()

    def gradient(chunk, first, count):
        return lax.dot_general(
            left[core, first * CELLS : (first + count) * CELLS],
            right[
                core,
                first * SIDE : (first + count) * SIDE,
                :,
                chunk * PART : (chunk + 1) * PART,
            ].reshape(count * CELLS, PART),
            (((0,), (0,)), ((), ())),
            preferred_element_type=F32,
        )

    def along(axis, o):
        if axis == 0:
            at = (x + o) & 3
            return (at << 2) | z, me_d, at
        if axis == 1:
            at = (z + o) & 3
            return (x << 2) | at, me_d, at
        at = (y + o) & 3
        return me_t, (at << 1) | core, at

    here = (x, z, y)
    orders = ((0, 1, 2), (1, 2, 0), (2, 0, 1))

    def piece1(chunk, part, at):
        lanes = slice(part * C, (part + 1) * C)
        if part == 0:
            return mine[chunk, at, :, :, :, lanes]
        if part == 1:
            return mine[chunk, :, at, :, :, lanes]
        return mine[chunk, :, :, at, :, lanes]

    s1_copies = [[], [], []]

    def step1(chunk):
        if chunk == 0:
            total = gradient(chunk, 0, 2 * NP - 1)
            for copy in pair_copies[NP - 1]:
                copy.wait()
            total = total + gradient(chunk, 2 * NP - 1, 1)
        else:
            total = gradient(chunk, 0, 2 * NP)
        mine[chunk] = total.reshape(AX, AX, AX, 8, PART)
        for o in (2, 1, 3):
            for part in range(3):
                tile, dp, at = along(orders[part][0], o)
                n = chunk * 9 + part * 3 + o - 1
                s1_send[n] = piece1(chunk, part, at).reshape(128, C).astype(BF16)
                copy = remote(
                    s1_send.at[n], s1_recv.at[n], s1_ssem.at[n], s1_rsem.at[n], tile, dp
                )
                copy.start()
                s1_copies[part].append(copy)

    for chunk in range(3):
        step1(chunk)

    def piece2(part, at):
        return tot2[part, :, at] if part == 1 else tot2[part, at]

    s2_copies = []
    for part in range(3):
        for copy in s1_copies[part]:
            copy.wait()
        for chunk in range(3):
            total = piece1(chunk, part, here[orders[part][0]])
            for o in range(3):
                landed = s1_recv[chunk * 9 + part * 3 + o].astype(F32)
                total = total + landed.reshape(AX, AX, 8, C)
            tot2[part, :, :, :, chunk * C : (chunk + 1) * C] = total
        row = []
        for o in (2, 1, 3):
            tile, dp, at = along(orders[part][1], o)
            n = part * 3 + o - 1
            s2_send[n] = piece2(part, at).reshape(32, PART).astype(BF16)
            copy = remote(s2_send.at[n], s2_recv.at[n], s2_ssem.at[n], s2_rsem.at[n], tile, dp)
            copy.start()
            row.append(copy)
        s2_copies.append(row)

    s3_copies = []
    for part in range(3):
        for copy in s2_copies[part]:
            copy.wait()
        total = piece2(part, here[orders[part][1]])
        for o in range(3):
            total = total + s2_recv[part * 3 + o].astype(F32).reshape(AX, 8, PART)
        tot3[part] = total
        row = []
        for o in (2, 1, 3):
            tile, dp, at = along(orders[part][2], o)
            n = part * 3 + o - 1
            copy = remote(
                tot3.at[part, at], s3_recv.at[n], s3_ssem.at[n], s3_rsem.at[n], tile, dp
            )
            copy.start()
            row.append(copy)
        s3_copies.append(row)

    squares = jnp.zeros((8, C), F32)
    for part in range(3):
        for copy in s3_copies[part]:
            copy.wait()
        total = tot3[part, here[orders[part][2]]]
        for o in range(3):
            total = total + s3_recv[part * 3 + o]
        for i in range(3):
            piece = total[:, i * C : (i + 1) * C]
            fin[0, :, (3 * i + part) * C : (3 * i + part + 1) * C] = piece
            squares = squares + piece * piece

    nrm_send[...] = squares
    nrm_recv[0] = squares
    copies = []
    for o in range(1, N_TILE):
        copy = remote(nrm_send, nrm_recv.at[o], n1_ssem.at[o], n1_rsem.at[o], tile_peer(o), me_d)
        copy.start()
        copies.append(copy)
    fin_copy = remote(fin.at[0], fin.at[1], fin_sem.at[0], fin_sem.at[1], me_t, sib)
    fin_copy.start()
    for copy in copies:
        copy.wait()
    plane = jnp.sum(nrm_recv[...], axis=0)
    nrm2_send[...] = plane
    nrm2_recv[me_d] = plane
    copies = []
    for o in range(1, N_DP):
        copy = remote(
            nrm2_send, nrm2_recv.at[me_d], n2_ssem.at[o], n2_rsem.at[o], me_t, dp_peer(o)
        )
        copy.start()
        copies.append(copy)
    fin_copy.wait()
    for copy in copies:
        copy.wait()

    total_a = jnp.sum(nrm2_recv[0] + nrm2_recv[2] + nrm2_recv[4] + nrm2_recv[6], keepdims=True)
    total_b = jnp.sum(nrm2_recv[1] + nrm2_recv[3] + nrm2_recv[5] + nrm2_recv[7], keepdims=True)
    root_a = jnp.sqrt(total_a / (HID * WIDE) + EPSILON)
    root_b = jnp.sqrt(total_b / (HID * WIDE) + EPSILON)
    full_a = fin[core] / root_a
    full_b = fin[1 - core] / root_b
    first = core == 0
    upda_ref[...] = jnp.where(first, full_a[0:4], full_a[4:8])
    updb_ref[...] = jnp.where(first, full_b[0:4], full_b[4:8])


def leave(a_in, b_in, c_in, a_out, b_out, c_out, sem):
    pairs = ((a_in, a_out), (b_in, b_out), (c_in, c_out))
    copies = [pltpu.make_async_copy(s, d, sem.at[i]) for i, (s, d) in enumerate(pairs)]
    for copy in copies:
        copy.start()
    for copy in copies:
        copy.wait()


def local(features, target_field, owner_tile, *rest):
    vmem = pl.BlockSpec(memory_space=pltpu.VMEM)
    smem = pl.BlockSpec(memory_space=pltpu.SMEM)
    hbm = pl.BlockSpec(memory_space=pl.ANY)
    dma = pltpu.SemaphoreType.DMA
    ints = pltpu.SMEM((NP,), jnp.int32)
    scratch = [
        ints,
        ints,
        ints,
        ints,
        ints,
        pltpu.VMEM((64, 256, C), BF16),
        pltpu.VMEM((64, 256, C), F32),
        pltpu.VMEM((64, 256), BF16),
        pltpu.VMEM((2, 64, C), F32),
        pltpu.VMEM((NP, SIDE, SIDE), F32),
        pltpu.VMEM((NP, SIDE, C), F32),
        pltpu.VMEM((TAPS, HID), F32),
        pltpu.VMEM((HID,), F32),
        pltpu.VMEM((HID,), F32),
        pltpu.VMEM((C,), F32),
        pltpu.VMEM((C,), F32),
        pltpu.VMEM((1, C), jnp.int32),
        pltpu.VMEM((N_TILE, 1, C), jnp.int32),
        pltpu.SMEM((N_TILE, 1, C), jnp.int32),
        pltpu.VMEM((6, 65, SIDE, C), BF16),
        pltpu.VMEM((2, AX, 65, SIDE, C), BF16),
        pltpu.VMEM((8, NP, 9, SIDE, C), BF16),
        pltpu.VMEM((2, AX, 9, SIDE, C), BF16),
        pltpu.VMEM((2, AX, 9, SIDE, C), BF16),
        pltpu.VMEM((2, AX, 9, SIDE, C), BF16),
        pltpu.VMEM((2, AX, 9, SIDE, C), BF16),
        pltpu.VMEM((SIDE, SIDE, C), BF16),
        pltpu.VMEM((WIDE + C, HID), BF16),
        pltpu.VMEM((C, HID), F32),
        pltpu.VMEM((HID, WIDE), BF16),
        pltpu.VMEM((2, 2 * NP * CELLS, HID), BF16),
        pltpu.VMEM((2, 2 * NP * SIDE, SIDE, WIDE + C), BF16),
        pltpu.VMEM((CELLS, HID), F32),
        pltpu.VMEM((3, AX, AX, AX, 8, PART), F32),
        pltpu.VMEM((27, 128, C), BF16),
        pltpu.VMEM((27, 128, C), BF16),
        pltpu.VMEM((3, AX, AX, 8, PART), F32),
        pltpu.VMEM((9, 32, PART), BF16),
        pltpu.VMEM((9, 32, PART), BF16),
        pltpu.VMEM((3, AX, 8, PART), F32),
        pltpu.VMEM((9, 8, PART), F32),
        pltpu.VMEM((2, 8, WIDE), F32),
        pltpu.VMEM((8, C), F32),
        pltpu.VMEM((N_TILE, 8, C), F32),
        pltpu.VMEM((8, C), F32),
        pltpu.VMEM((N_DP, 8, C), F32),
        dma((32,)),
        dma((N_TILE,)),
        dma((N_TILE,)),
        dma((6,)),
        dma((6,)),
        dma((32,)),
        dma((32,)),
        dma((2 * NP,)),
        dma((2 * NP,)),
        dma((27,)),
        dma((27,)),
        dma((9,)),
        dma((9,)),
        dma((9,)),
        dma((9,)),
        dma((2,)),
        dma((N_TILE,)),
        dma((N_TILE,)),
        dma((N_DP,)),
        dma((N_DP,)),
    ]
    outs = (
        jax.ShapeDtypeStruct((NP,), F32),
        jax.ShapeDtypeStruct((4, WIDE), F32),
        jax.ShapeDtypeStruct((4, WIDE), F32),
    )
    results = pl.pallas_call(
        kernel,
        out_shape=outs,
        in_specs=[hbm] * 15,
        out_specs=(smem, vmem, vmem),
        scratch_shapes=scratch,
        compiler_params=pltpu.CompilerParams(
            collective_id=0, has_side_effects=True, vmem_limit_bytes=60 * 2**20
        ),
    )(features, target_field, owner_tile.reshape(-1), *rest)
    return pl.pallas_call(
        leave,
        out_shape=outs,
        in_specs=[hbm] * 3,
        out_specs=(hbm,) * 3,
        scratch_shapes=[dma((3,))],
    )(*results)


def solution(mesh):
    both = ("tile", "dp")
    return jax.shard_map(
        local,
        mesh=mesh,
        in_specs=(
            P("tile", None, None),
            P("tile", None),
            P(both, None),
            P(both),
            P(both),
            P(both),
            P(both),
            P(both, None, None),
            P(),
            P(),
            P(),
            P(),
            P(),
            P(),
            P(),
        ),
        out_specs=(P(both), P(both, None), P(both, None)),
        check_vma=False,
    )
```

```python
import functools
import math

import jax
import jax.numpy as jnp
from jax import lax
from jax.experimental import pallas as pl
from jax.experimental.pallas import tpu as pltpu
from jax.sharding import PartitionSpec as P

C = 128
HID = 512
SIDE = 16
LEVELS = 32
NP = 4
CELLS = SIDE * SIDE
TAPS = 9
WIDE = TAPS * C
SIGMA_LOW = 0.02
SIGMA_HIGH = 80.0
SIGMA_DATA = 0.5
EPSILON = 1e-06
LOG_LOW = math.log(SIGMA_LOW)
LOG_STEP = (math.log(SIGMA_HIGH) - math.log(SIGMA_LOW)) / (LEVELS - 1)

MESH = pl.DeviceIdType.MESH
F32 = jnp.float32
BF16 = jnp.bfloat16
N_TILE = 16
N_DP = 8
AX = 4
PART = WIDE // 3


def iota(shape, dim):
    return lax.broadcasted_iota(jnp.int32, shape, dim)


def remote(src, dst, send_sem, recv_sem, tile, dp):
    return pltpu.make_async_remote_copy(
        src_ref=src,
        dst_ref=dst,
        send_sem=send_sem,
        recv_sem=recv_sem,
        device_id=(tile, dp),
        device_id_type=MESH,
    )


def column_shifts(block):
    col = iota(block.shape, 1)
    before = jnp.where(col == 0, 0.0, pltpu.roll(block, 1, axis=1))
    after = jnp.where(col == SIDE - 1, 0.0, pltpu.roll(block, SIDE - 1, axis=1))
    return before, block, after


def store_rows(dst, p, lane, rows, delta):
    lanes = pl.ds(lane, C)
    base = p * SIDE
    zero = jnp.zeros((1, SIDE, C), BF16)
    if delta == 0:
        dst[base : base + SIDE, :, lanes] = rows
    elif delta < 0:
        dst[base : base + 1, :, lanes] = zero
        dst[base + 1 : base + SIDE, :, lanes] = rows[: SIDE - 1]
    else:
        dst[base : base + SIDE - 1, :, lanes] = rows[1:]
        dst[base + SIDE - 1 : base + SIDE, :, lanes] = zero


def kernel(
    feat_hbm,
    tgt_hbm,
    owner_hbm,
    row_hbm,
    col_hbm,
    level_hbm,
    count_hbm,
    noise_hbm,
    wa_hbm,
    wu_hbm,
    ba_hbm,
    ea_hbm,
    wb_hbm,
    bb_hbm,
    wo_hbm,
    losses_ref,
    upda_ref,
    updb_ref,
    owner_ref,
    row_ref,
    col_ref,
    level_ref,
    count_ref,
    feat_v,
    feat_f,
    tgt_b,
    tgt_v,
    noise_b,
    noise_v,
    wu_ref,
    ba_ref,
    ea_ref,
    bb_ref,
    wo_ref,
    req_send,
    req_recv,
    req_smem,
    m1_send,
    m1_recv,
    m2_send,
    m2_recv0,
    m2_recv1,
    m2_recv2,
    m2_recv3,
    blk,
    wfull,
    wext,
    w2,
    left,
    right,
    slope,
    raw_send,
    raw_recv,
    mine,
    s1_send,
    s1_recv,
    tot2,
    s2_send,
    s2_recv,
    tot3,
    s3_recv,
    fin,
    nrm_send,
    nrm_recv,
    nrm2_send,
    nrm2_recv,
    local_sem,
    req_ssem,
    req_rsem,
    m1_ssem,
    m1_rsem,
    m2_ssem,
    m2_rsem,
    sib_ssem,
    sib_rsem,
    s1_ssem,
    s1_rsem,
    s2_ssem,
    s2_rsem,
    s3_ssem,
    s3_rsem,
    fin_sem,
    n1_ssem,
    n1_rsem,
    n2_ssem,
    n2_rsem,
):
    me_t = lax.axis_index("tile")
    me_d = lax.axis_index("dp")
    x, z = me_t >> 2, me_t & 3
    y, core = me_d >> 1, me_d & 1

    def tile_at(dx, dz):
        return (((x + dx) & 3) << 2) | ((z + dz) & 3)

    def tile_peer(o):
        return tile_at(o >> 2, o & 3)

    def dp_peer(o):
        return (me_d + o) & (N_DP - 1)

    m2_recv = (m2_recv0, m2_recv1, m2_recv2, m2_recv3)

    barrier = pltpu.get_barrier_semaphore()
    staged = []

    def stage(src, dst):
        copy = pltpu.make_async_copy(src, dst, local_sem.at[len(staged)])
        copy.start()
        staged.append(copy)
        return copy

    ints = [
        stage(a, b)
        for a, b in (
            (owner_hbm, owner_ref),
            (row_hbm, row_ref),
            (col_hbm, col_ref),
            (level_hbm, level_ref),
            (count_hbm, count_ref),
        )
    ]
    for o in range(1, N_TILE):
        pl.semaphore_signal(barrier, inc=1, device_id=(tile_peer(o), me_d), device_id_type=MESH)
    for o in range(1, N_DP):
        pl.semaphore_signal(barrier, inc=1, device_id=(me_t, dp_peer(o)), device_id_type=MESH)

    feat_copy = stage(feat_hbm, feat_v)
    tgt_copy = stage(tgt_hbm, tgt_b)
    small = [
        stage(a, b)
        for a, b in (
            (noise_hbm, noise_b),
            (wu_hbm, wu_ref),
            (ba_hbm, ba_ref),
            (ea_hbm, ea_ref),
            (bb_hbm, bb_ref),
            (wo_hbm, wo_ref),
        )
    ]
    small.append(stage(wa_hbm, wfull.at[pl.ds(0, WIDE)]))
    for t in range(TAPS):
        small.append(stage(wb_hbm.at[pl.ds(t * HID, HID)], w2.at[:, pl.ds(t * C, C)]))
    for copy in ints:
        copy.wait()

    lane = iota((1, C), 1)
    line = jnp.zeros((1, C), jnp.int32)
    for k in range(NP):
        line = jnp.where(lane == 4 * k, owner_ref[k], line)
        line = jnp.where(lane == 4 * k + 1, row_ref[k], line)
        line = jnp.where(lane == 4 * k + 2, col_ref[k], line)
    req_send[...] = line
    req_recv[me_t] = line
    pl.semaphore_wait(barrier, N_TILE - 1 + N_DP - 1)

    copies = []
    for o in range(1, N_TILE):
        copy = remote(
            req_send, req_recv.at[me_t], req_ssem.at[o], req_rsem.at[o], tile_peer(o), me_d
        )
        copy.start()
        copies.append(copy)

    tgt_copy.wait()
    tgt_v[0] = tgt_b[:, :C].astype(F32)
    tgt_v[1] = tgt_b[:, C:].astype(F32)
    feat_copy.wait()

    @pl.loop(0, 32)
    def _(i):
        feat_f[2 * i] = feat_v[2 * i].astype(F32)
        feat_f[2 * i + 1] = feat_v[2 * i + 1].astype(F32)

    for copy in copies:
        copy.wait()
    to_smem = pltpu.make_async_copy(req_recv, req_smem, local_sem.at[len(staged)])
    to_smem.start()
    to_smem.wait()

    lane2 = iota((SIDE, C), 1)

    def turn(value, shift):
        amount = jnp.full(value.shape, shift & (C - 1), jnp.int32)
        for bit in (1, 2, 4, 8, 16, 32, 64):
            value = jnp.where((amount & bit) != 0, pltpu.roll(value, bit, axis=1), value)
        return value

    def wanted(j):
        rank = jnp.int32(0)
        rows = [jnp.int32(0), jnp.int32(0)]
        cols = [jnp.int32(0), jnp.int32(0)]
        for k in range(NP):
            hit = req_smem[j, 0, 4 * k] == me_t
            for q in range(2):
                take = hit & (rank == q)
                rows[q] = jnp.where(take, req_smem[j, 0, 4 * k + 1], rows[q])
                cols[q] = jnp.where(take, req_smem[j, 0, 4 * k + 2], cols[q])
            rank = rank + hit.astype(jnp.int32)
        return rows, cols

    def fill(half, o, dst):
        def one(e, tile):
            rows, cols = wanted(tile_at(e, o) if half == 0 else tile_at(o, e))
            for q in range(2):
                block = feat_f[pl.ds(rows[q] + 8 * half, 8), pl.ds(cols[q], SIDE), :]
                dst[pl.ds((2 * e + q) * 8, 8)] = block.astype(BF16)
                if half == 0:
                    high = cols[q] >> 7
                    shift = cols[q] & (C - 1)
                    low_part = tgt_v[high, pl.ds(rows[q], SIDE), :]
                    next_part = tgt_v[1, pl.ds(rows[q], SIDE), :]
                    both = jnp.where(lane2 < shift, next_part, low_part)
                    both = turn(both, (2 * e + q) * SIDE - shift)
                    tile = jnp.where((lane2 >> 4) == 2 * e + q, both, tile)
            return tile

        tile = lax.fori_loop(0, AX, one, jnp.zeros((SIDE, C), F32), unroll=True)
        if half == 0:
            dst[64] = tile.astype(BF16)

    m1_copies = ([], [])
    for o in (2, 1, 3):
        for half in range(2):
            n = 3 * half + o - 1
            fill(half, o, m1_send.at[n])
            units = 65 - half
            copy = remote(
                m1_send.at[n, pl.ds(0, units)],
                m1_recv.at[half, o, pl.ds(0, units)],
                m1_ssem.at[n],
                m1_rsem.at[n],
                tile_at(0, o) if half == 0 else tile_at(o, 0),
                me_d,
            )
            copy.start()
            m1_copies[half].append(copy)
    for half in range(2):
        fill(half, 0, m1_recv.at[half, 0])

    for copy in small:
        copy.wait()
    wu = wu_ref[...]
    wu_hi = wu.astype(BF16).astype(F32)
    ba = ba_ref[...].reshape(1, HID)
    ba_hi = ba.astype(BF16).astype(F32)
    ea = ea_ref[...].reshape(1, HID)
    ea_hi = ea.astype(BF16).astype(F32)
    wext[...] = jnp.zeros_like(wext)
    wext[0:9] = wu_hi
    wext[9:18] = wu - wu_hi
    wext[18:27] = wu_hi
    wext[27:28] = ba_hi
    wext[28:29] = ba - ba_hi
    wext[29:30] = ea_hi
    wext[30:31] = ea - ea_hi
    wext[31:32] = ea_hi
    wfull[WIDE:, :] = wext[...].astype(BF16)
    noise_v[...] = jnp.zeros_like(noise_v)
    noise_v[:, :, 0:SIDE] = noise_b[...]

    for half in range(2):
        for copy in m1_copies[half]:
            copy.wait()

    def rank_of(j, k):
        rank = jnp.int32(0)
        for before in range(k):
            same = req_smem[j, 0, 4 * before] == req_smem[j, 0, 4 * k]
            rank = rank + same.astype(jnp.int32)
        return jnp.minimum(rank, 1)

    m2_copies = []
    for k in range(NP):
        row = []
        for e in (2, 1, 3, 0):
            for half in range(2):
                j = tile_at(e, 0) if half == 0 else tile_at(0, e)
                owner = req_smem[j, 0, 4 * k]
                rank = rank_of(j, k)
                if half == 0:
                    o = (z - (owner & 3)) & 3
                else:
                    o = (x - (owner >> 2)) & 3
                if e:
                    dst = m2_send.at[half * 4 + e, k]
                else:
                    dst = m2_recv[k].at[half, 0]
                dst[0:8] = m1_recv[half, o, pl.ds((2 * e + rank) * 8, 8)]
                if half == 0:
                    tile = m1_recv[0, o, 64].astype(F32)
                    if e:
                        tile = pltpu.roll(tile, C - 2 * e * SIDE, axis=1)
                    second = jnp.full(tile.shape, rank, jnp.int32) != 0
                    tile = jnp.where(second, pltpu.roll(tile, C - SIDE, axis=1), tile)
                    dst[8] = tile.astype(BF16)
                if e:
                    units = 9 - half
                    n = half * 16 + e * 4 + k
                    copy = remote(
                        m2_send.at[half * 4 + e, k, pl.ds(0, units)],
                        m2_recv[k].at[half, e, pl.ds(0, units)],
                        m2_ssem.at[n],
                        m2_rsem.at[n],
                        j,
                        me_d,
                    )
                    copy.start()
                    row.append(copy)
        m2_copies.append(row)

    sib = me_d ^ 1
    pair_copies = []
    wo = wo_ref[...].reshape(1, 1, C)
    bb = bb_ref[...].reshape(1, 1, C)
    shape3 = (SIDE, SIDE, C)
    col3, lane3 = iota(shape3, 1), iota(shape3, 2)
    none = jnp.zeros((1, SIDE, C), F32)
    for p in range(NP):
        for copy in m2_copies[p]:
            copy.wait()
        owner = owner_ref[p]
        from_x, from_z = (x - (owner >> 2)) & 3, (z - (owner & 3)) & 3
        blk[0:8] = m2_recv[p][0, from_x, 0:8]
        blk[8:16] = m2_recv[p][1, from_z, 0:8]
        clean = jnp.where(lane2 < SIDE, m2_recv[p][0, from_x, 8].astype(F32), 0.0)
        xcol = right.at[0]
        gcol = right.at[1]
        block = blk[...].astype(F32)
        for s, moved in enumerate(column_shifts(block)):
            rows = moved.astype(BF16)
            for r in range(3):
                store_rows(xcol, p, (3 * r + s) * C, rows, r - 1)

        level = jnp.full((SIDE, C), level_ref[p], jnp.int32).astype(F32)
        sigma = jnp.exp(LOG_LOW + level * LOG_STEP)
        variance = sigma * sigma + SIGMA_DATA * SIGMA_DATA
        scale_in = 1.0 / jnp.sqrt(variance)
        scale_skip = SIGMA_DATA * SIGMA_DATA / variance
        scale_out = sigma * SIGMA_DATA * scale_in
        embed = jnp.log(sigma) / 4.0
        noisy = clean + sigma * noise_v[p]
        aim = (clean - scale_skip * noisy) / scale_out
        scaled = pltpu.roll(scale_in * noisy, 1, axis=1)
        wide = jnp.broadcast_to(scaled[:, None, :], shape3)
        for bit in (1, 2, 4, 8):
            wide = jnp.where((col3 & bit) != 0, pltpu.roll(wide, C - bit, axis=2), wide)
        wide = jnp.where(lane3 < 3, wide, 0.0)
        taps = (
            jnp.concatenate([none, wide[: SIDE - 1]], axis=0)
            + pltpu.roll(wide, 3, axis=2)
            + pltpu.roll(jnp.concatenate([wide[1:], none], axis=0), 6, axis=2)
        )
        taps_hi = taps.astype(BF16).astype(F32)
        emb = embed[0:1, :][None]
        emb_hi = emb.astype(BF16).astype(F32)
        extra = taps_hi + pltpu.roll(taps_hi, 9, axis=2) + pltpu.roll(taps - taps_hi, 18, axis=2)
        extra = jnp.where((lane3 == 27) | (lane3 == 28), 1.0, extra)
        extra = jnp.where((lane3 == 29) | (lane3 == 30), emb_hi, extra)
        extra = jnp.where(lane3 == 31, emb - emb_hi, extra)
        xcol[p * SIDE : (p + 1) * SIDE, :, WIDE:] = extra.astype(BF16)

        cells = slice(p * CELLS, (p + 1) * CELLS)
        window = xcol[p * SIDE : (p + 1) * SIDE].reshape(CELLS, WIDE + C)
        pre_a = jnp.dot(window, wfull[...], preferred_element_type=F32)
        gate = jax.nn.sigmoid(pre_a)
        slope[...] = gate * (1.0 + pre_a * (1.0 - gate))
        hidden = (pre_a * gate).astype(BF16)
        left[1, cells] = hidden

        spread = jnp.dot(hidden, w2[...], preferred_element_type=F32).reshape(SIDE, SIDE, WIDE)

        def tap_rows(s):
            up = spread[:, :, s * C : (s + 1) * C]
            mid = spread[:, :, (3 + s) * C : (4 + s) * C]
            down = spread[:, :, (6 + s) * C : (7 + s) * C]
            return (
                mid
                + jnp.concatenate([none, up[: SIDE - 1]], axis=0)
                + jnp.concatenate([down[1:], none], axis=0)
            )

        before = jnp.where(col3 == 0, 0.0, pltpu.roll(tap_rows(0), 1, axis=1))
        after = jnp.where(col3 == SIDE - 1, 0.0, pltpu.roll(tap_rows(2), SIDE - 1, axis=1))
        pre_b = bb + tap_rows(1) + before + after
        gate_b = jax.nn.sigmoid(pre_b)
        aim3 = jnp.where(col3 == lane3, jnp.broadcast_to(aim[:, None, :], shape3), 0.0)
        residual = jnp.sum(pre_b * gate_b * wo - aim3, axis=2, keepdims=True)
        weight = count_ref[p].astype(F32)
        losses_ref[p] = jnp.sum(residual * residual) * weight / CELLS
        grad_final = (2.0 * weight / CELLS) * residual
        grad_b = grad_final * wo * (gate_b * (1.0 + pre_b * (1.0 - gate_b)))
        grad_b = grad_b.astype(BF16).astype(F32)
        raw_send[p] = jnp.where(core == 0, grad_b, block).astype(BF16)
        for s, moved in enumerate(column_shifts(grad_b)):
            rows = moved.astype(BF16)
            for r in range(3):
                store_rows(gcol, p, (3 * (2 - r) + (2 - s)) * C, rows, r - 1)

        back = lax.dot_general(
            gcol[p * SIDE : (p + 1) * SIDE, :, 0:WIDE].reshape(CELLS, WIDE),
            w2[...],
            (((1,), (1,)), ((), ())),
            preferred_element_type=F32,
        )
        left[0, cells] = (back * slope[...]).astype(BF16)

        row = []
        for i, src, dst in (
            (0, raw_send.at[p], raw_recv.at[p]),
            (
                1,
                left.at[1 - core, pl.ds(p * CELLS, CELLS)],
                left.at[1 - core, pl.ds((NP + p) * CELLS, CELLS)],
            ),
        ):
            copy = remote(
                src, dst, sib_ssem.at[2 * p + i], sib_rsem.at[2 * p + i], me_t, sib
            )
            copy.start()
            row.append(copy)
        pair_copies.append(row)

    def sibling_columns(p):
        for copy in pair_copies[p]:
            copy.wait()
        dst = right.at[core]
        for s, moved in enumerate(column_shifts(raw_recv[p].astype(F32))):
            rows = moved.astype(BF16)
            for r in range(3):
                tap = 3 * r + s
                lane = pl.multiple_of(jnp.where(core == 0, tap, TAPS - 1 - tap) * C, C)
                store_rows(dst, NP + p, lane, rows, r - 1)

    for p in range(NP - 1):
        sibling_columns(p)

    def gradient(chunk, first, count):
        return lax.dot_general(
            left[core, first * CELLS : (first + count) * CELLS],
            right[
                core,
                first * SIDE : (first + count) * SIDE,
                :,
                chunk * PART : (chunk + 1) * PART,
            ].reshape(count * CELLS, PART),
            (((0,), (0,)), ((), ())),
            preferred_element_type=F32,
        )

    def along(axis, o):
        if axis == 0:
            at = (x + o) & 3
            return (at << 2) | z, me_d, at
        if axis == 1:
            at = (z + o) & 3
            return (x << 2) | at, me_d, at
        at = (y + o) & 3
        return me_t, (at << 1) | core, at

    here = (x, z, y)
    orders = ((0, 1, 2), (1, 2, 0), (2, 0, 1))

    def piece1(chunk, part, at):
        lanes = slice(part * C, (part + 1) * C)
        if part == 0:
            return mine[chunk, at, :, :, :, lanes]
        if part == 1:
            return mine[chunk, :, at, :, :, lanes]
        return mine[chunk, :, :, at, :, lanes]

    s1_copies = [[], [], []]

    def step1(chunk):
        if chunk == 0:
            total = gradient(chunk, 0, 2 * NP - 1)
            sibling_columns(NP - 1)
            total = total + gradient(chunk, 2 * NP - 1, 1)
        else:
            total = gradient(chunk, 0, 2 * NP)
        mine[chunk] = total.reshape(AX, AX, AX, 8, PART)
        for o in (2, 1, 3):
            for part in range(3):
                tile, dp, at = along(orders[part][0], o)
                n = chunk * 9 + part * 3 + o - 1
                s1_send[n] = piece1(chunk, part, at).reshape(128, C).astype(BF16)
                copy = remote(
                    s1_send.at[n], s1_recv.at[n], s1_ssem.at[n], s1_rsem.at[n], tile, dp
                )
                copy.start()
                s1_copies[part].append(copy)

    for chunk in range(3):
        step1(chunk)

    def piece2(part, at):
        return tot2[part, :, at] if part == 1 else tot2[part, at]

    s2_copies = []
    for part in range(3):
        for copy in s1_copies[part]:
            copy.wait()
        for chunk in range(3):
            total = piece1(chunk, part, here[orders[part][0]])
            for o in range(3):
                landed = s1_recv[chunk * 9 + part * 3 + o].astype(F32)
                total = total + landed.reshape(AX, AX, 8, C)
            tot2[part, :, :, :, chunk * C : (chunk + 1) * C] = total
        row = []
        for o in (2, 1, 3):
            tile, dp, at = along(orders[part][1], o)
            n = part * 3 + o - 1
            s2_send[n] = piece2(part, at).reshape(32, PART).astype(BF16)
            copy = remote(s2_send.at[n], s2_recv.at[n], s2_ssem.at[n], s2_rsem.at[n], tile, dp)
            copy.start()
            row.append(copy)
        s2_copies.append(row)

    s3_copies = []
    for part in range(3):
        for copy in s2_copies[part]:
            copy.wait()
        total = piece2(part, here[orders[part][1]])
        for o in range(3):
            total = total + s2_recv[part * 3 + o].astype(F32).reshape(AX, 8, PART)
        tot3[part] = total
        row = []
        for o in (2, 1, 3):
            tile, dp, at = along(orders[part][2], o)
            n = part * 3 + o - 1
            copy = remote(
                tot3.at[part, at], s3_recv.at[n], s3_ssem.at[n], s3_rsem.at[n], tile, dp
            )
            copy.start()
            row.append(copy)
        s3_copies.append(row)

    squares = jnp.zeros((8, C), F32)
    for part in range(3):
        for copy in s3_copies[part]:
            copy.wait()
        total = tot3[part, here[orders[part][2]]]
        for o in range(3):
            total = total + s3_recv[part * 3 + o]
        for i in range(3):
            piece = total[:, i * C : (i + 1) * C]
            fin[0, :, (3 * i + part) * C : (3 * i + part + 1) * C] = piece
            squares = squares + piece * piece

    nrm_send[...] = squares
    nrm_recv[0] = squares
    copies = []
    for o in range(1, N_TILE):
        copy = remote(nrm_send, nrm_recv.at[o], n1_ssem.at[o], n1_rsem.at[o], tile_peer(o), me_d)
        copy.start()
        copies.append(copy)
    fin_copy = remote(fin.at[0], fin.at[1], fin_sem.at[0], fin_sem.at[1], me_t, sib)
    fin_copy.start()
    for copy in copies:
        copy.wait()
    plane = jnp.sum(nrm_recv[...], axis=0)
    nrm2_send[...] = plane
    nrm2_recv[me_d] = plane
    copies = []
    for o in range(1, N_DP):
        copy = remote(
            nrm2_send, nrm2_recv.at[me_d], n2_ssem.at[o], n2_rsem.at[o], me_t, dp_peer(o)
        )
        copy.start()
        copies.append(copy)
    fin_copy.wait()
    for copy in copies:
        copy.wait()

    total_a = jnp.sum(nrm2_recv[0] + nrm2_recv[2] + nrm2_recv[4] + nrm2_recv[6], keepdims=True)
    total_b = jnp.sum(nrm2_recv[1] + nrm2_recv[3] + nrm2_recv[5] + nrm2_recv[7], keepdims=True)
    root_a = jnp.sqrt(total_a / (HID * WIDE) + EPSILON)
    root_b = jnp.sqrt(total_b / (HID * WIDE) + EPSILON)
    full_a = fin[core] / root_a
    full_b = fin[1 - core] / root_b
    first = core == 0
    upda_ref[...] = jnp.where(first, full_a[0:4], full_a[4:8])
    updb_ref[...] = jnp.where(first, full_b[0:4], full_b[4:8])


def leave(a_in, b_in, c_in, a_out, b_out, c_out, sem):
    pairs = ((a_in, a_out), (b_in, b_out), (c_in, c_out))
    copies = [pltpu.make_async_copy(s, d, sem.at[i]) for i, (s, d) in enumerate(pairs)]
    for copy in copies:
        copy.start()
    for copy in copies:
        copy.wait()


def local(features, target_field, owner_tile, *rest):
    vmem = pl.BlockSpec(memory_space=pltpu.VMEM)
    smem = pl.BlockSpec(memory_space=pltpu.SMEM)
    hbm = pl.BlockSpec(memory_space=pl.ANY)
    dma = pltpu.SemaphoreType.DMA
    ints = pltpu.SMEM((NP,), jnp.int32)
    scratch = [
        ints,
        ints,
        ints,
        ints,
        ints,
        pltpu.VMEM((64, 256, C), BF16),
        pltpu.VMEM((64, 256, C), F32),
        pltpu.VMEM((64, 256), BF16),
        pltpu.VMEM((2, 64, C), F32),
        pltpu.VMEM((NP, SIDE, SIDE), F32),
        pltpu.VMEM((NP, SIDE, C), F32),
        pltpu.VMEM((TAPS, HID), F32),
        pltpu.VMEM((HID,), F32),
        pltpu.VMEM((HID,), F32),
        pltpu.VMEM((C,), F32),
        pltpu.VMEM((C,), F32),
        pltpu.VMEM((1, C), jnp.int32),
        pltpu.VMEM((N_TILE, 1, C), jnp.int32),
        pltpu.SMEM((N_TILE, 1, C), jnp.int32),
        pltpu.VMEM((6, 65, SIDE, C), BF16),
        pltpu.VMEM((2, AX, 65, SIDE, C), BF16),
        pltpu.VMEM((8, NP, 9, SIDE, C), BF16),
        pltpu.VMEM((2, AX, 9, SIDE, C), BF16),
        pltpu.VMEM((2, AX, 9, SIDE, C), BF16),
        pltpu.VMEM((2, AX, 9, SIDE, C), BF16),
        pltpu.VMEM((2, AX, 9, SIDE, C), BF16),
        pltpu.VMEM((SIDE, SIDE, C), BF16),
        pltpu.VMEM((WIDE + C, HID), BF16),
        pltpu.VMEM((C, HID), F32),
        pltpu.VMEM((HID, WIDE), BF16),
        pltpu.VMEM((2, 2 * NP * CELLS, HID), BF16),
        pltpu.VMEM((2, 2 * NP * SIDE, SIDE, WIDE + C), BF16),
        pltpu.VMEM((CELLS, HID), F32),
        pltpu.VMEM((NP, SIDE, SIDE, C), BF16),
        pltpu.VMEM((NP, SIDE, SIDE, C), BF16),
        pltpu.VMEM((3, AX, AX, AX, 8, PART), F32),
        pltpu.VMEM((27, 128, C), BF16),
        pltpu.VMEM((27, 128, C), BF16),
        pltpu.VMEM((3, AX, AX, 8, PART), F32),
        pltpu.VMEM((9, 32, PART), BF16),
        pltpu.VMEM((9, 32, PART), BF16),
        pltpu.VMEM((3, AX, 8, PART), F32),
        pltpu.VMEM((9, 8, PART), F32),
        pltpu.VMEM((2, 8, WIDE), F32),
        pltpu.VMEM((8, C), F32),
        pltpu.VMEM((N_TILE, 8, C), F32),
        pltpu.VMEM((8, C), F32),
        pltpu.VMEM((N_DP, 8, C), F32),
        dma((32,)),
        dma((N_TILE,)),
        dma((N_TILE,)),
        dma((6,)),
        dma((6,)),
        dma((32,)),
        dma((32,)),
        dma((2 * NP,)),
        dma((2 * NP,)),
        dma((27,)),
        dma((27,)),
        dma((9,)),
        dma((9,)),
        dma((9,)),
        dma((9,)),
        dma((2,)),
        dma((N_TILE,)),
        dma((N_TILE,)),
        dma((N_DP,)),
        dma((N_DP,)),
    ]
    outs = (
        jax.ShapeDtypeStruct((NP,), F32),
        jax.ShapeDtypeStruct((4, WIDE), F32),
        jax.ShapeDtypeStruct((4, WIDE), F32),
    )
    results = pl.pallas_call(
        kernel,
        out_shape=(outs[0], pltpu.VMEM((4, WIDE), F32), pltpu.VMEM((4, WIDE), F32)),
        in_specs=[hbm] * 15,
        out_specs=(smem, vmem, vmem),
        scratch_shapes=scratch,
        compiler_params=pltpu.CompilerParams(
            collective_id=0, has_side_effects=True, vmem_limit_bytes=60 * 2**20
        ),
    )(features, target_field, owner_tile.reshape(-1), *rest)
    return pl.pallas_call(
        leave,
        out_shape=outs,
        in_specs=[hbm, vmem, vmem],
        out_specs=(hbm,) * 3,
        scratch_shapes=[dma((3,))],
    )(results[0], *[pltpu.with_memory_space_constraint(a, pltpu.VMEM) for a in results[1:]])


def solution(mesh):
    both = ("tile", "dp")
    return jax.shard_map(
        local,
        mesh=mesh,
        in_specs=(
            P("tile", None, None),
            P("tile", None),
            P(both, None),
            P(both),
            P(both),
            P(both),
            P(both),
            P(both, None, None),
            P(),
            P(),
            P(),
            P(),
            P(),
            P(),
            P(),
        ),
        out_specs=(P(both), P(both, None), P(both, None)),
        check_vma=False,
    )
```

```python
import functools
import math

import jax
import jax.numpy as jnp
from jax import lax
from jax.experimental import pallas as pl
from jax.experimental.pallas import tpu as pltpu
from jax.sharding import PartitionSpec as P

C = 128
HID = 512
SIDE = 16
LEVELS = 32
NP = 4
CELLS = SIDE * SIDE
TAPS = 9
WIDE = TAPS * C
SIGMA_LOW = 0.02
SIGMA_HIGH = 80.0
SIGMA_DATA = 0.5
EPSILON = 1e-06
LOG_LOW = math.log(SIGMA_LOW)
LOG_STEP = (math.log(SIGMA_HIGH) - math.log(SIGMA_LOW)) / (LEVELS - 1)

MESH = pl.DeviceIdType.MESH
F32 = jnp.float32
BF16 = jnp.bfloat16
N_TILE = 16
N_DP = 8
AX = 4
PART = WIDE // 3


def iota(shape, dim):
    return lax.broadcasted_iota(jnp.int32, shape, dim)


def remote(src, dst, send_sem, recv_sem, tile, dp):
    return pltpu.make_async_remote_copy(
        src_ref=src,
        dst_ref=dst,
        send_sem=send_sem,
        recv_sem=recv_sem,
        device_id=(tile, dp),
        device_id_type=MESH,
    )


def column_shifts(block):
    col = iota(block.shape, 1)
    before = jnp.where(col == 0, 0.0, pltpu.roll(block, 1, axis=1))
    after = jnp.where(col == SIDE - 1, 0.0, pltpu.roll(block, SIDE - 1, axis=1))
    return before, block, after


def store_rows(dst, p, lane, rows, delta):
    lanes = pl.ds(lane, C)
    base = p * SIDE
    zero = jnp.zeros((1, SIDE, C), BF16)
    if delta == 0:
        dst[base : base + SIDE, :, lanes] = rows
    elif delta < 0:
        dst[base : base + 1, :, lanes] = zero
        dst[base + 1 : base + SIDE, :, lanes] = rows[: SIDE - 1]
    else:
        dst[base : base + SIDE - 1, :, lanes] = rows[1:]
        dst[base + SIDE - 1 : base + SIDE, :, lanes] = zero


def kernel(
    feat_hbm,
    tgt_hbm,
    owner_hbm,
    row_hbm,
    col_hbm,
    level_hbm,
    count_hbm,
    noise_hbm,
    wa_hbm,
    wu_hbm,
    ba_hbm,
    ea_hbm,
    wb_hbm,
    bb_hbm,
    wo_hbm,
    losses_ref,
    upda_ref,
    updb_ref,
    owner_ref,
    row_ref,
    col_ref,
    level_ref,
    count_ref,
    feat_v,
    feat_f,
    tgt_b,
    tgt_v,
    noise_b,
    noise_v,
    wu_ref,
    ba_ref,
    ea_ref,
    bb_ref,
    wo_ref,
    req_send,
    req_recv,
    req_smem,
    m1_send,
    m1_recv,
    m2_send,
    m2_recv0,
    m2_recv1,
    m2_recv2,
    m2_recv3,
    blk,
    wfull,
    wext,
    w2,
    left,
    right,
    slope,
    raw_send,
    raw_recv,
    mine,
    s1_send,
    s1_recv,
    tot2,
    s2_send,
    s2_recv,
    tot3,
    s3_recv,
    fin,
    nrm_send,
    nrm_recv,
    nrm2_send,
    nrm2_recv,
    local_sem,
    req_ssem,
    req_rsem,
    m1_ssem,
    m1_rsem,
    m2_ssem,
    m2_rsem,
    sib_ssem,
    sib_rsem,
    s1_ssem,
    s1_rsem,
    s2_ssem,
    s2_rsem,
    s3_ssem,
    s3_rsem,
    fin_sem,
    n1_ssem,
    n1_rsem,
    n2_ssem,
    n2_rsem,
):
    me_t = lax.axis_index("tile")
    me_d = lax.axis_index("dp")
    x, z = me_t >> 2, me_t & 3
    y, core = me_d >> 1, me_d & 1

    def tile_at(dx, dz):
        return (((x + dx) & 3) << 2) | ((z + dz) & 3)

    def tile_peer(o):
        return tile_at(o >> 2, o & 3)

    def dp_peer(o):
        return (me_d + o) & (N_DP - 1)

    m2_recv = (m2_recv0, m2_recv1, m2_recv2, m2_recv3)

    barrier = pltpu.get_barrier_semaphore()
    staged = []

    def stage(src, dst):
        copy = pltpu.make_async_copy(src, dst, local_sem.at[len(staged)])
        copy.start()
        staged.append(copy)
        return copy

    ints = [
        stage(a, b)
        for a, b in (
            (owner_hbm, owner_ref),
            (row_hbm, row_ref),
            (col_hbm, col_ref),
            (level_hbm, level_ref),
            (count_hbm, count_ref),
        )
    ]
    for o in range(1, N_TILE):
        pl.semaphore_signal(barrier, inc=1, device_id=(tile_peer(o), me_d), device_id_type=MESH)
    for o in range(1, N_DP):
        pl.semaphore_signal(barrier, inc=1, device_id=(me_t, dp_peer(o)), device_id_type=MESH)

    feat_copy = stage(feat_hbm, feat_v)
    tgt_copy = stage(tgt_hbm, tgt_b)
    small = [
        stage(a, b)
        for a, b in (
            (noise_hbm, noise_b),
            (wu_hbm, wu_ref),
            (ba_hbm, ba_ref),
            (ea_hbm, ea_ref),
            (bb_hbm, bb_ref),
            (wo_hbm, wo_ref),
        )
    ]
    small.append(stage(wa_hbm, wfull.at[pl.ds(0, WIDE)]))
    for t in range(TAPS):
        small.append(stage(wb_hbm.at[pl.ds(t * HID, HID)], w2.at[:, pl.ds(t * C, C)]))
    for copy in ints:
        copy.wait()

    lane = iota((1, C), 1)
    line = jnp.zeros((1, C), jnp.int32)
    for k in range(NP):
        line = jnp.where(lane == 4 * k, owner_ref[k], line)
        line = jnp.where(lane == 4 * k + 1, row_ref[k], line)
        line = jnp.where(lane == 4 * k + 2, col_ref[k], line)
    req_send[...] = line
    req_recv[me_t] = line
    pl.semaphore_wait(barrier, N_TILE - 1 + N_DP - 1)

    copies = []
    for o in range(1, N_TILE):
        copy = remote(
            req_send, req_recv.at[me_t], req_ssem.at[o], req_rsem.at[o], tile_peer(o), me_d
        )
        copy.start()
        copies.append(copy)

    tgt_copy.wait()
    tgt_v[0] = tgt_b[:, :C].astype(F32)
    tgt_v[1] = tgt_b[:, C:].astype(F32)
    feat_copy.wait()

    @pl.loop(0, 32)
    def _(i):
        feat_f[2 * i] = feat_v[2 * i].astype(F32)
        feat_f[2 * i + 1] = feat_v[2 * i + 1].astype(F32)

    for copy in copies:
        copy.wait()
    to_smem = pltpu.make_async_copy(req_recv, req_smem, local_sem.at[len(staged)])
    to_smem.start()
    to_smem.wait()

    lane2 = iota((SIDE, C), 1)

    def turn(value, shift):
        amount = jnp.full(value.shape, shift & (C - 1), jnp.int32)
        for bit in (1, 2, 4, 8, 16, 32, 64):
            value = jnp.where((amount & bit) != 0, pltpu.roll(value, bit, axis=1), value)
        return value

    def wanted(j):
        rank = jnp.int32(0)
        rows = [jnp.int32(0), jnp.int32(0)]
        cols = [jnp.int32(0), jnp.int32(0)]
        for k in range(NP):
            hit = req_smem[j, 0, 4 * k] == me_t
            for q in range(2):
                take = hit & (rank == q)
                rows[q] = jnp.where(take, req_smem[j, 0, 4 * k + 1], rows[q])
                cols[q] = jnp.where(take, req_smem[j, 0, 4 * k + 2], cols[q])
            rank = rank + hit.astype(jnp.int32)
        return rows, cols

    def fill(half, o, dst):
        def one(e, tile):
            rows, cols = wanted(tile_at(e, o) if half == 0 else tile_at(o, e))
            for q in range(2):
                block = feat_f[pl.ds(rows[q] + 8 * half, 8), pl.ds(cols[q], SIDE), :]
                dst[pl.ds((2 * e + q) * 8, 8)] = block.astype(BF16)
                if half == 0:
                    high = cols[q] >> 7
                    shift = cols[q] & (C - 1)
                    low_part = tgt_v[high, pl.ds(rows[q], SIDE), :]
                    next_part = tgt_v[1, pl.ds(rows[q], SIDE), :]
                    both = jnp.where(lane2 < shift, next_part, low_part)
                    both = turn(both, (2 * e + q) * SIDE - shift)
                    tile = jnp.where((lane2 >> 4) == 2 * e + q, both, tile)
            return tile

        tile = lax.fori_loop(0, AX, one, jnp.zeros((SIDE, C), F32), unroll=True)
        if half == 0:
            dst[64] = tile.astype(BF16)

    m1_copies = ([], [])
    for o in (2, 1, 3):
        for half in range(2):
            n = 3 * half + o - 1
            fill(half, o, m1_send.at[n])
            units = 65 - half
            copy = remote(
                m1_send.at[n, pl.ds(0, units)],
                m1_recv.at[half, o, pl.ds(0, units)],
                m1_ssem.at[n],
                m1_rsem.at[n],
                tile_at(0, o) if half == 0 else tile_at(o, 0),
                me_d,
            )
            copy.start()
            m1_copies[half].append(copy)
    for half in range(2):
        fill(half, 0, m1_recv.at[half, 0])

    for copy in small:
        copy.wait()
    wu = wu_ref[...]
    wu_hi = wu.astype(BF16).astype(F32)
    ba = ba_ref[...].reshape(1, HID)
    ba_hi = ba.astype(BF16).astype(F32)
    ea = ea_ref[...].reshape(1, HID)
    ea_hi = ea.astype(BF16).astype(F32)
    wext[...] = jnp.zeros_like(wext)
    wext[0:9] = wu_hi
    wext[9:18] = wu - wu_hi
    wext[18:27] = wu_hi
    wext[27:28] = ba_hi
    wext[28:29] = ba - ba_hi
    wext[29:30] = ea_hi
    wext[30:31] = ea - ea_hi
    wext[31:32] = ea_hi
    wfull[WIDE:, :] = wext[...].astype(BF16)
    noise_v[...] = jnp.zeros_like(noise_v)
    noise_v[:, :, 0:SIDE] = noise_b[...]

    for half in range(2):
        for copy in m1_copies[half]:
            copy.wait()

    def rank_of(j, k):
        rank = jnp.int32(0)
        for before in range(k):
            same = req_smem[j, 0, 4 * before] == req_smem[j, 0, 4 * k]
            rank = rank + same.astype(jnp.int32)
        return jnp.minimum(rank, 1)

    m2_copies = [[] for _ in range(NP)]
    order = [(k, e) for k in range(NP) for e in (2, 1, 3)] + [(k, 0) for k in range(NP)]
    for k, e in order:
        for half in range(2):
            j = tile_at(e, 0) if half == 0 else tile_at(0, e)
            owner = req_smem[j, 0, 4 * k]
            rank = rank_of(j, k)
            if half == 0:
                o = (z - (owner & 3)) & 3
            else:
                o = (x - (owner >> 2)) & 3
            if e:
                dst = m2_send.at[half * 4 + e, k]
            else:
                dst = m2_recv[k].at[half, 0]
            dst[0:8] = m1_recv[half, o, pl.ds((2 * e + rank) * 8, 8)]
            if half == 0:
                tile = m1_recv[0, o, 64].astype(F32)
                if e:
                    tile = pltpu.roll(tile, C - 2 * e * SIDE, axis=1)
                second = jnp.full(tile.shape, rank, jnp.int32) != 0
                tile = jnp.where(second, pltpu.roll(tile, C - SIDE, axis=1), tile)
                dst[8] = tile.astype(BF16)
            if e:
                units = 9 - half
                n = half * 16 + e * 4 + k
                copy = remote(
                    m2_send.at[half * 4 + e, k, pl.ds(0, units)],
                    m2_recv[k].at[half, e, pl.ds(0, units)],
                    m2_ssem.at[n],
                    m2_rsem.at[n],
                    j,
                    me_d,
                )
                copy.start()
                m2_copies[k].append(copy)

    sib = me_d ^ 1
    pair_copies = []
    wo = wo_ref[...].reshape(1, 1, C)
    bb = bb_ref[...].reshape(1, 1, C)
    shape3 = (SIDE, SIDE, C)
    col3, lane3 = iota(shape3, 1), iota(shape3, 2)
    none = jnp.zeros((1, SIDE, C), F32)
    for p in range(NP):
        for copy in m2_copies[p]:
            copy.wait()
        owner = owner_ref[p]
        from_x, from_z = (x - (owner >> 2)) & 3, (z - (owner & 3)) & 3
        blk[0:8] = m2_recv[p][0, from_x, 0:8]
        blk[8:16] = m2_recv[p][1, from_z, 0:8]
        clean = jnp.where(lane2 < SIDE, m2_recv[p][0, from_x, 8].astype(F32), 0.0)
        xcol = right.at[0]
        gcol = right.at[1]
        block = blk[...].astype(F32)
        for s, moved in enumerate(column_shifts(block)):
            rows = moved.astype(BF16)
            for r in range(3):
                store_rows(xcol, p, (3 * r + s) * C, rows, r - 1)

        level = jnp.full((SIDE, C), level_ref[p], jnp.int32).astype(F32)
        sigma = jnp.exp(LOG_LOW + level * LOG_STEP)
        variance = sigma * sigma + SIGMA_DATA * SIGMA_DATA
        scale_in = 1.0 / jnp.sqrt(variance)
        scale_skip = SIGMA_DATA * SIGMA_DATA / variance
        scale_out = sigma * SIGMA_DATA * scale_in
        embed = jnp.log(sigma) / 4.0
        noisy = clean + sigma * noise_v[p]
        aim = (clean - scale_skip * noisy) / scale_out
        scaled = pltpu.roll(scale_in * noisy, 1, axis=1)
        wide = jnp.broadcast_to(scaled[:, None, :], shape3)
        for bit in (1, 2, 4, 8):
            wide = jnp.where((col3 & bit) != 0, pltpu.roll(wide, C - bit, axis=2), wide)
        wide = jnp.where(lane3 < 3, wide, 0.0)
        taps = (
            jnp.concatenate([none, wide[: SIDE - 1]], axis=0)
            + pltpu.roll(wide, 3, axis=2)
            + pltpu.roll(jnp.concatenate([wide[1:], none], axis=0), 6, axis=2)
        )
        taps_hi = taps.astype(BF16).astype(F32)
        emb = embed[0:1, :][None]
        emb_hi = emb.astype(BF16).astype(F32)
        extra = taps_hi + pltpu.roll(taps_hi, 9, axis=2) + pltpu.roll(taps - taps_hi, 18, axis=2)
        extra = jnp.where((lane3 == 27) | (lane3 == 28), 1.0, extra)
        extra = jnp.where((lane3 == 29) | (lane3 == 30), emb_hi, extra)
        extra = jnp.where(lane3 == 31, emb - emb_hi, extra)
        xcol[p * SIDE : (p + 1) * SIDE, :, WIDE:] = extra.astype(BF16)

        cells = slice(p * CELLS, (p + 1) * CELLS)
        window = xcol[p * SIDE : (p + 1) * SIDE].reshape(CELLS, WIDE + C)
        pre_a = jnp.dot(window, wfull[...], preferred_element_type=F32)
        gate = jax.nn.sigmoid(pre_a)
        slope[...] = gate * (1.0 + pre_a * (1.0 - gate))
        hidden = (pre_a * gate).astype(BF16)
        left[1, cells] = hidden

        spread = jnp.dot(hidden, w2[...], preferred_element_type=F32).reshape(SIDE, SIDE, WIDE)

        def tap_rows(s):
            up = spread[:, :, s * C : (s + 1) * C]
            mid = spread[:, :, (3 + s) * C : (4 + s) * C]
            down = spread[:, :, (6 + s) * C : (7 + s) * C]
            return (
                mid
                + jnp.concatenate([none, up[: SIDE - 1]], axis=0)
                + jnp.concatenate([down[1:], none], axis=0)
            )

        before = jnp.where(col3 == 0, 0.0, pltpu.roll(tap_rows(0), 1, axis=1))
        after = jnp.where(col3 == SIDE - 1, 0.0, pltpu.roll(tap_rows(2), SIDE - 1, axis=1))
        pre_b = bb + tap_rows(1) + before + after
        gate_b = jax.nn.sigmoid(pre_b)
        aim3 = jnp.where(col3 == lane3, jnp.broadcast_to(aim[:, None, :], shape3), 0.0)
        residual = jnp.sum(pre_b * gate_b * wo - aim3, axis=2, keepdims=True)
        weight = count_ref[p].astype(F32)
        losses_ref[p] = jnp.sum(residual * residual) * weight / CELLS
        grad_final = (2.0 * weight / CELLS) * residual
        grad_b = grad_final * wo * (gate_b * (1.0 + pre_b * (1.0 - gate_b)))
        grad_b = grad_b.astype(BF16).astype(F32)
        raw_send[p] = jnp.where(core == 0, grad_b, block).astype(BF16)
        for s, moved in enumerate(column_shifts(grad_b)):
            rows = moved.astype(BF16)
            for r in range(3):
                store_rows(gcol, p, (3 * (2 - r) + (2 - s)) * C, rows, r - 1)

        back = lax.dot_general(
            gcol[p * SIDE : (p + 1) * SIDE, :, 0:WIDE].reshape(CELLS, WIDE),
            w2[...],
            (((1,), (1,)), ((), ())),
            preferred_element_type=F32,
        )
        left[0, cells] = (back * slope[...]).astype(BF16)

        row = []
        for i, src, dst in (
            (0, raw_send.at[p], raw_recv.at[p]),
            (
                1,
                left.at[1 - core, pl.ds(p * CELLS, CELLS)],
                left.at[1 - core, pl.ds((NP + p) * CELLS, CELLS)],
            ),
        ):
            copy = remote(
                src, dst, sib_ssem.at[2 * p + i], sib_rsem.at[2 * p + i], me_t, sib
            )
            copy.start()
            row.append(copy)
        pair_copies.append(row)

    def sibling_columns(p):
        for copy in pair_copies[p]:
            copy.wait()
        dst = right.at[core]
        for s, moved in enumerate(column_shifts(raw_recv[p].astype(F32))):
            rows = moved.astype(BF16)
            for r in range(3):
                tap = 3 * r + s
                lane = pl.multiple_of(jnp.where(core == 0, tap, TAPS - 1 - tap) * C, C)
                store_rows(dst, NP + p, lane, rows, r - 1)

    for p in range(NP - 1):
        sibling_columns(p)

    def gradient(chunk, first, count):
        return lax.dot_general(
            left[core, first * CELLS : (first + count) * CELLS],
            right[
                core,
                first * SIDE : (first + count) * SIDE,
                :,
                chunk * PART : (chunk + 1) * PART,
            ].reshape(count * CELLS, PART),
            (((0,), (0,)), ((), ())),
            preferred_element_type=F32,
        )

    def along(axis, o):
        if axis == 0:
            at = (x + o) & 3
            return (at << 2) | z, me_d, at
        if axis == 1:
            at = (z + o) & 3
            return (x << 2) | at, me_d, at
        at = (y + o) & 3
        return me_t, (at << 1) | core, at

    here = (x, z, y)
    orders = ((0, 1, 2), (1, 2, 0), (2, 0, 1))

    def piece1(chunk, part, at):
        lanes = slice(part * C, (part + 1) * C)
        if part == 0:
            return mine[chunk, at, :, :, :, lanes]
        if part == 1:
            return mine[chunk, :, at, :, :, lanes]
        return mine[chunk, :, :, at, :, lanes]

    s1_copies = [[], [], []]

    def put(chunk, total):
        mine[chunk] = total.reshape(AX, AX, AX, 8, PART)

    def add(chunk, total):
        mine[chunk] = mine[chunk] + total.reshape(AX, AX, AX, 8, PART)

    def step1(chunk):
        for o in (2, 1, 3):
            for part in range(3):
                tile, dp, at = along(orders[part][0], o)
                n = chunk * 9 + part * 3 + o - 1
                s1_send[n] = piece1(chunk, part, at).reshape(128, C).astype(BF16)
                copy = remote(
                    s1_send.at[n], s1_recv.at[n], s1_ssem.at[n], s1_rsem.at[n], tile, dp
                )
                copy.start()
                s1_copies[part].append(copy)

    for chunk in range(2):
        put(chunk, gradient(chunk, 0, 2 * NP - 1))
    sibling_columns(NP - 1)
    for chunk in range(2):
        add(chunk, gradient(chunk, 2 * NP - 1, 1))
        step1(chunk)
    put(2, gradient(2, 0, 2 * NP))
    step1(2)

    def piece2(part, at):
        return tot2[part, :, at] if part == 1 else tot2[part, at]

    s2_copies = []
    for part in range(3):
        for copy in s1_copies[part]:
            copy.wait()
        for chunk in range(3):
            total = piece1(chunk, part, here[orders[part][0]])
            for o in range(3):
                landed = s1_recv[chunk * 9 + part * 3 + o].astype(F32)
                total = total + landed.reshape(AX, AX, 8, C)
            tot2[part, :, :, :, chunk * C : (chunk + 1) * C] = total
        row = []
        for o in (2, 1, 3):
            tile, dp, at = along(orders[part][1], o)
            n = part * 3 + o - 1
            s2_send[n] = piece2(part, at).reshape(32, PART).astype(BF16)
            copy = remote(s2_send.at[n], s2_recv.at[n], s2_ssem.at[n], s2_rsem.at[n], tile, dp)
            copy.start()
            row.append(copy)
        s2_copies.append(row)

    s3_copies = []
    for part in range(3):
        for copy in s2_copies[part]:
            copy.wait()
        total = piece2(part, here[orders[part][1]])
        for o in range(3):
            total = total + s2_recv[part * 3 + o].astype(F32).reshape(AX, 8, PART)
        tot3[part] = total
        row = []
        for o in (2, 1, 3):
            tile, dp, at = along(orders[part][2], o)
            n = part * 3 + o - 1
            copy = remote(
                tot3.at[part, at], s3_recv.at[n], s3_ssem.at[n], s3_rsem.at[n], tile, dp
            )
            copy.start()
            row.append(copy)
        s3_copies.append(row)

    squares = jnp.zeros((8, C), F32)
    for part in range(3):
        for copy in s3_copies[part]:
            copy.wait()
        total = tot3[part, here[orders[part][2]]]
        for o in range(3):
            total = total + s3_recv[part * 3 + o]
        for i in range(3):
            piece = total[:, i * C : (i + 1) * C]
            fin[0, :, (3 * i + part) * C : (3 * i + part + 1) * C] = piece
            squares = squares + piece * piece

    nrm_send[...] = squares
    nrm_recv[0] = squares
    copies = []
    for o in range(1, N_TILE):
        copy = remote(nrm_send, nrm_recv.at[o], n1_ssem.at[o], n1_rsem.at[o], tile_peer(o), me_d)
        copy.start()
        copies.append(copy)
    fin_copy = remote(fin.at[0], fin.at[1], fin_sem.at[0], fin_sem.at[1], me_t, sib)
    fin_copy.start()
    for copy in copies:
        copy.wait()
    plane = jnp.sum(nrm_recv[...], axis=0)
    nrm2_send[...] = plane
    nrm2_recv[me_d] = plane
    copies = []
    for o in range(1, N_DP):
        copy = remote(
            nrm2_send, nrm2_recv.at[me_d], n2_ssem.at[o], n2_rsem.at[o], me_t, dp_peer(o)
        )
        copy.start()
        copies.append(copy)
    fin_copy.wait()
    for copy in copies:
        copy.wait()

    total_a = jnp.sum(nrm2_recv[0] + nrm2_recv[2] + nrm2_recv[4] + nrm2_recv[6], keepdims=True)
    total_b = jnp.sum(nrm2_recv[1] + nrm2_recv[3] + nrm2_recv[5] + nrm2_recv[7], keepdims=True)
    root_a = jnp.sqrt(total_a / (HID * WIDE) + EPSILON)
    root_b = jnp.sqrt(total_b / (HID * WIDE) + EPSILON)
    full_a = fin[core] / root_a
    full_b = fin[1 - core] / root_b
    first = core == 0
    upda_ref[...] = jnp.where(first, full_a[0:4], full_a[4:8])
    updb_ref[...] = jnp.where(first, full_b[0:4], full_b[4:8])


def leave(a_in, b_in, c_in, a_out, b_out, c_out, sem):
    pairs = ((a_in, a_out), (b_in, b_out), (c_in, c_out))
    copies = [pltpu.make_async_copy(s, d, sem.at[i]) for i, (s, d) in enumerate(pairs)]
    for copy in copies:
        copy.start()
    for copy in copies:
        copy.wait()


def local(features, target_field, owner_tile, *rest):
    vmem = pl.BlockSpec(memory_space=pltpu.VMEM)
    smem = pl.BlockSpec(memory_space=pltpu.SMEM)
    hbm = pl.BlockSpec(memory_space=pl.ANY)
    dma = pltpu.SemaphoreType.DMA
    ints = pltpu.SMEM((NP,), jnp.int32)
    scratch = [
        ints,
        ints,
        ints,
        ints,
        ints,
        pltpu.VMEM((64, 256, C), BF16),
        pltpu.VMEM((64, 256, C), F32),
        pltpu.VMEM((64, 256), BF16),
        pltpu.VMEM((2, 64, C), F32),
        pltpu.VMEM((NP, SIDE, SIDE), F32),
        pltpu.VMEM((NP, SIDE, C), F32),
        pltpu.VMEM((TAPS, HID), F32),
        pltpu.VMEM((HID,), F32),
        pltpu.VMEM((HID,), F32),
        pltpu.VMEM((C,), F32),
        pltpu.VMEM((C,), F32),
        pltpu.VMEM((1, C), jnp.int32),
        pltpu.VMEM((N_TILE, 1, C), jnp.int32),
        pltpu.SMEM((N_TILE, 1, C), jnp.int32),
        pltpu.VMEM((6, 65, SIDE, C), BF16),
        pltpu.VMEM((2, AX, 65, SIDE, C), BF16),
        pltpu.VMEM((8, NP, 9, SIDE, C), BF16),
        pltpu.VMEM((2, AX, 9, SIDE, C), BF16),
        pltpu.VMEM((2, AX, 9, SIDE, C), BF16),
        pltpu.VMEM((2, AX, 9, SIDE, C), BF16),
        pltpu.VMEM((2, AX, 9, SIDE, C), BF16),
        pltpu.VMEM((SIDE, SIDE, C), BF16),
        pltpu.VMEM((WIDE + C, HID), BF16),
        pltpu.VMEM((C, HID), F32),
        pltpu.VMEM((HID, WIDE), BF16),
        pltpu.VMEM((2, 2 * NP * CELLS, HID), BF16),
        pltpu.VMEM((2, 2 * NP * SIDE, SIDE, WIDE + C), BF16),
        pltpu.VMEM((CELLS, HID), F32),
        pltpu.VMEM((NP, SIDE, SIDE, C), BF16),
        pltpu.VMEM((NP, SIDE, SIDE, C), BF16),
        pltpu.VMEM((3, AX, AX, AX, 8, PART), F32),
        pltpu.VMEM((27, 128, C), BF16),
        pltpu.VMEM((27, 128, C), BF16),
        pltpu.VMEM((3, AX, AX, 8, PART), F32),
        pltpu.VMEM((9, 32, PART), BF16),
        pltpu.VMEM((9, 32, PART), BF16),
        pltpu.VMEM((3, AX, 8, PART), F32),
        pltpu.VMEM((9, 8, PART), F32),
        pltpu.VMEM((2, 8, WIDE), F32),
        pltpu.VMEM((8, C), F32),
        pltpu.VMEM((N_TILE, 8, C), F32),
        pltpu.VMEM((8, C), F32),
        pltpu.VMEM((N_DP, 8, C), F32),
        dma((32,)),
        dma((N_TILE,)),
        dma((N_TILE,)),
        dma((6,)),
        dma((6,)),
        dma((32,)),
        dma((32,)),
        dma((2 * NP,)),
        dma((2 * NP,)),
        dma((27,)),
        dma((27,)),
        dma((9,)),
        dma((9,)),
        dma((9,)),
        dma((9,)),
        dma((2,)),
        dma((N_TILE,)),
        dma((N_TILE,)),
        dma((N_DP,)),
        dma((N_DP,)),
    ]
    outs = (
        jax.ShapeDtypeStruct((NP,), F32),
        jax.ShapeDtypeStruct((4, WIDE), F32),
        jax.ShapeDtypeStruct((4, WIDE), F32),
    )
    results = pl.pallas_call(
        kernel,
        out_shape=(outs[0], pltpu.VMEM((4, WIDE), F32), pltpu.VMEM((4, WIDE), F32)),
        in_specs=[hbm] * 15,
        out_specs=(smem, vmem, vmem),
        scratch_shapes=scratch,
        compiler_params=pltpu.CompilerParams(
            collective_id=0, has_side_effects=True, vmem_limit_bytes=60 * 2**20
        ),
    )(features, target_field, owner_tile.reshape(-1), *rest)
    return pl.pallas_call(
        leave,
        out_shape=outs,
        in_specs=[hbm, vmem, vmem],
        out_specs=(hbm,) * 3,
        scratch_shapes=[dma((3,))],
    )(results[0], *[pltpu.with_memory_space_constraint(a, pltpu.VMEM) for a in results[1:]])


def solution(mesh):
    both = ("tile", "dp")
    return jax.shard_map(
        local,
        mesh=mesh,
        in_specs=(
            P("tile", None, None),
            P("tile", None),
            P(both, None),
            P(both),
            P(both),
            P(both),
            P(both),
            P(both, None, None),
            P(),
            P(),
            P(),
            P(),
            P(),
            P(),
            P(),
        ),
        out_specs=(P(both), P(both, None), P(both, None)),
        check_vma=False,
    )
```

```python
import functools
import math

import jax
import jax.numpy as jnp
from jax import lax
from jax.experimental import pallas as pl
from jax.experimental.pallas import tpu as pltpu
from jax.sharding import PartitionSpec as P

C = 128
HID = 512
SIDE = 16
LEVELS = 32
NP = 4
CELLS = SIDE * SIDE
TAPS = 9
WIDE = TAPS * C
SIGMA_LOW = 0.02
SIGMA_HIGH = 80.0
SIGMA_DATA = 0.5
EPSILON = 1e-06
LOG_LOW = math.log(SIGMA_LOW)
LOG_STEP = (math.log(SIGMA_HIGH) - math.log(SIGMA_LOW)) / (LEVELS - 1)

MESH = pl.DeviceIdType.MESH
F32 = jnp.float32
BF16 = jnp.bfloat16
N_TILE = 16
N_DP = 8
AX = 4
PART = WIDE // 3


def iota(shape, dim):
    return lax.broadcasted_iota(jnp.int32, shape, dim)


def remote(src, dst, send_sem, recv_sem, tile, dp):
    return pltpu.make_async_remote_copy(
        src_ref=src,
        dst_ref=dst,
        send_sem=send_sem,
        recv_sem=recv_sem,
        device_id=(tile, dp),
        device_id_type=MESH,
    )


def column_shifts(block):
    col = iota(block.shape, 1)
    before = jnp.where(col == 0, 0.0, pltpu.roll(block, 1, axis=1))
    after = jnp.where(col == SIDE - 1, 0.0, pltpu.roll(block, SIDE - 1, axis=1))
    return before, block, after


def store_rows(dst, p, lane, rows, delta):
    lanes = pl.ds(lane, C)
    base = p * SIDE
    zero = jnp.zeros((1, SIDE, C), BF16)
    if delta == 0:
        dst[base : base + SIDE, :, lanes] = rows
    elif delta < 0:
        dst[base : base + 1, :, lanes] = zero
        dst[base + 1 : base + SIDE, :, lanes] = rows[: SIDE - 1]
    else:
        dst[base : base + SIDE - 1, :, lanes] = rows[1:]
        dst[base + SIDE - 1 : base + SIDE, :, lanes] = zero


def kernel(
    feat_hbm,
    tgt_hbm,
    owner_hbm,
    row_hbm,
    col_hbm,
    level_hbm,
    count_hbm,
    noise_hbm,
    wa_hbm,
    wu_hbm,
    ba_hbm,
    ea_hbm,
    wb_hbm,
    bb_hbm,
    wo_hbm,
    losses_ref,
    upda_ref,
    updb_ref,
    owner_ref,
    row_ref,
    col_ref,
    level_ref,
    count_ref,
    feat_v,
    feat_f,
    tgt_b,
    tgt_v,
    noise_b,
    noise_v,
    wu_ref,
    ba_ref,
    ea_ref,
    bb_ref,
    wo_ref,
    req_send,
    req_recv,
    req_smem,
    m1_send,
    m1_recv,
    m2_send,
    m2_recv0,
    m2_recv1,
    m2_recv2,
    m2_recv3,
    blk,
    wfull,
    wext,
    w2,
    left,
    right,
    slope,
    raw_send,
    raw_recv,
    mine,
    s1_send,
    s1_recv,
    tot2,
    s2_send,
    s2_recv,
    tot3,
    s3_recv,
    fin,
    nrm_send,
    nrm_recv,
    nrm2_send,
    nrm2_recv,
    local_sem,
    req_ssem,
    req_rsem,
    m1_ssem,
    m1_rsem,
    m2_ssem,
    m2_rsem,
    sib_ssem,
    sib_rsem,
    s1_ssem,
    s1_rsem,
    s2_ssem,
    s2_rsem,
    s3_ssem,
    s3_rsem,
    fin_sem,
    n1_ssem,
    n1_rsem,
    n2_ssem,
    n2_rsem,
):
    me_t = lax.axis_index("tile")
    me_d = lax.axis_index("dp")
    x, z = me_t >> 2, me_t & 3
    y, core = me_d >> 1, me_d & 1

    def tile_at(dx, dz):
        return (((x + dx) & 3) << 2) | ((z + dz) & 3)

    def tile_peer(o):
        return tile_at(o >> 2, o & 3)

    def dp_peer(o):
        return (me_d + o) & (N_DP - 1)

    m2_recv = (m2_recv0, m2_recv1, m2_recv2, m2_recv3)

    leaving = []

    def arrive(copies):
        for copy in copies:
            copy.wait_recv()
        leaving.extend(copies)

    def settle():
        for copy in leaving:
            copy.wait_send()
        leaving.clear()

    barrier = pltpu.get_barrier_semaphore()
    staged = []

    def stage(src, dst):
        copy = pltpu.make_async_copy(src, dst, local_sem.at[len(staged)])
        copy.start()
        staged.append(copy)
        return copy

    ints = [
        stage(a, b)
        for a, b in (
            (owner_hbm, owner_ref),
            (row_hbm, row_ref),
            (col_hbm, col_ref),
            (level_hbm, level_ref),
            (count_hbm, count_ref),
        )
    ]
    for o in range(1, N_TILE):
        pl.semaphore_signal(barrier, inc=1, device_id=(tile_peer(o), me_d), device_id_type=MESH)
    for o in range(1, N_DP):
        pl.semaphore_signal(barrier, inc=1, device_id=(me_t, dp_peer(o)), device_id_type=MESH)

    feat_copy = stage(feat_hbm, feat_v)
    tgt_copy = stage(tgt_hbm, tgt_b)
    small = [
        stage(a, b)
        for a, b in (
            (noise_hbm, noise_b),
            (wu_hbm, wu_ref),
            (ba_hbm, ba_ref),
            (ea_hbm, ea_ref),
            (bb_hbm, bb_ref),
            (wo_hbm, wo_ref),
        )
    ]
    small.append(stage(wa_hbm, wfull.at[pl.ds(0, WIDE)]))
    for t in range(TAPS):
        small.append(stage(wb_hbm.at[pl.ds(t * HID, HID)], w2.at[:, pl.ds(t * C, C)]))
    for copy in ints:
        copy.wait()

    lane = iota((1, C), 1)
    line = jnp.zeros((1, C), jnp.int32)
    for k in range(NP):
        line = jnp.where(lane == 4 * k, owner_ref[k], line)
        line = jnp.where(lane == 4 * k + 1, row_ref[k], line)
        line = jnp.where(lane == 4 * k + 2, col_ref[k], line)
    req_send[...] = line
    req_recv[me_t] = line
    pl.semaphore_wait(barrier, N_TILE - 1 + N_DP - 1)

    copies = []
    for o in range(1, N_TILE):
        copy = remote(
            req_send, req_recv.at[me_t], req_ssem.at[o], req_rsem.at[o], tile_peer(o), me_d
        )
        copy.start()
        copies.append(copy)

    tgt_copy.wait()
    tgt_v[0] = tgt_b[:, :C].astype(F32)
    tgt_v[1] = tgt_b[:, C:].astype(F32)
    feat_copy.wait()

    @pl.loop(0, 32)
    def _(i):
        feat_f[2 * i] = feat_v[2 * i].astype(F32)
        feat_f[2 * i + 1] = feat_v[2 * i + 1].astype(F32)

    arrive(copies)
    to_smem = pltpu.make_async_copy(req_recv, req_smem, local_sem.at[len(staged)])
    to_smem.start()
    to_smem.wait()

    lane2 = iota((SIDE, C), 1)

    def turn(value, shift):
        amount = jnp.full(value.shape, shift & (C - 1), jnp.int32)
        for bit in (1, 2, 4, 8, 16, 32, 64):
            value = jnp.where((amount & bit) != 0, pltpu.roll(value, bit, axis=1), value)
        return value

    def wanted(j):
        rank = jnp.int32(0)
        rows = [jnp.int32(0), jnp.int32(0)]
        cols = [jnp.int32(0), jnp.int32(0)]
        for k in range(NP):
            hit = req_smem[j, 0, 4 * k] == me_t
            for q in range(2):
                take = hit & (rank == q)
                rows[q] = jnp.where(take, req_smem[j, 0, 4 * k + 1], rows[q])
                cols[q] = jnp.where(take, req_smem[j, 0, 4 * k + 2], cols[q])
            rank = rank + hit.astype(jnp.int32)
        return rows, cols

    def fill(half, o, dst):
        def one(e, tile):
            rows, cols = wanted(tile_at(e, o) if half == 0 else tile_at(o, e))
            for q in range(2):
                block = feat_f[pl.ds(rows[q] + 8 * half, 8), pl.ds(cols[q], SIDE), :]
                dst[pl.ds((2 * e + q) * 8, 8)] = block.astype(BF16)
                if half == 0:
                    high = cols[q] >> 7
                    shift = cols[q] & (C - 1)
                    low_part = tgt_v[high, pl.ds(rows[q], SIDE), :]
                    next_part = tgt_v[1, pl.ds(rows[q], SIDE), :]
                    both = jnp.where(lane2 < shift, next_part, low_part)
                    both = turn(both, (2 * e + q) * SIDE - shift)
                    tile = jnp.where((lane2 >> 4) == 2 * e + q, both, tile)
            return tile

        tile = lax.fori_loop(0, AX, one, jnp.zeros((SIDE, C), F32), unroll=True)
        if half == 0:
            dst[64] = tile.astype(BF16)

    m1_copies = ([], [])
    for o in (2, 1, 3):
        for half in range(2):
            n = 3 * half + o - 1
            fill(half, o, m1_send.at[n])
            units = 65 - half
            copy = remote(
                m1_send.at[n, pl.ds(0, units)],
                m1_recv.at[half, o, pl.ds(0, units)],
                m1_ssem.at[n],
                m1_rsem.at[n],
                tile_at(0, o) if half == 0 else tile_at(o, 0),
                me_d,
            )
            copy.start()
            m1_copies[half].append(copy)
    for half in range(2):
        fill(half, 0, m1_recv.at[half, 0])
    settle()

    for copy in small:
        copy.wait()
    wu = wu_ref[...]
    wu_hi = wu.astype(BF16).astype(F32)
    ba = ba_ref[...].reshape(1, HID)
    ba_hi = ba.astype(BF16).astype(F32)
    ea = ea_ref[...].reshape(1, HID)
    ea_hi = ea.astype(BF16).astype(F32)
    wext[...] = jnp.zeros_like(wext)
    wext[0:9] = wu_hi
    wext[9:18] = wu - wu_hi
    wext[18:27] = wu_hi
    wext[27:28] = ba_hi
    wext[28:29] = ba - ba_hi
    wext[29:30] = ea_hi
    wext[30:31] = ea - ea_hi
    wext[31:32] = ea_hi
    wfull[WIDE:, :] = wext[...].astype(BF16)
    noise_v[...] = jnp.zeros_like(noise_v)
    noise_v[:, :, 0:SIDE] = noise_b[...]

    for half in range(2):
        arrive(m1_copies[half])

    def rank_of(j, k):
        rank = jnp.int32(0)
        for before in range(k):
            same = req_smem[j, 0, 4 * before] == req_smem[j, 0, 4 * k]
            rank = rank + same.astype(jnp.int32)
        return jnp.minimum(rank, 1)

    m2_copies = [[] for _ in range(NP)]
    order = [(k, e) for k in range(NP) for e in (2, 1, 3)] + [(k, 0) for k in range(NP)]
    for k, e in order:
        for half in range(2):
            j = tile_at(e, 0) if half == 0 else tile_at(0, e)
            owner = req_smem[j, 0, 4 * k]
            rank = rank_of(j, k)
            if half == 0:
                o = (z - (owner & 3)) & 3
            else:
                o = (x - (owner >> 2)) & 3
            if e:
                dst = m2_send.at[half * 4 + e, k]
            else:
                dst = m2_recv[k].at[half, 0]
            dst[0:8] = m1_recv[half, o, pl.ds((2 * e + rank) * 8, 8)]
            if half == 0:
                tile = m1_recv[0, o, 64].astype(F32)
                if e:
                    tile = pltpu.roll(tile, C - 2 * e * SIDE, axis=1)
                second = jnp.full(tile.shape, rank, jnp.int32) != 0
                tile = jnp.where(second, pltpu.roll(tile, C - SIDE, axis=1), tile)
                dst[8] = tile.astype(BF16)
            if e:
                units = 9 - half
                n = half * 16 + e * 4 + k
                copy = remote(
                    m2_send.at[half * 4 + e, k, pl.ds(0, units)],
                    m2_recv[k].at[half, e, pl.ds(0, units)],
                    m2_ssem.at[n],
                    m2_rsem.at[n],
                    j,
                    me_d,
                )
                copy.start()
                m2_copies[k].append(copy)

    settle()

    sib = me_d ^ 1
    pair_copies = []
    wo = wo_ref[...].reshape(1, 1, C)
    bb = bb_ref[...].reshape(1, 1, C)
    shape3 = (SIDE, SIDE, C)
    col3, lane3 = iota(shape3, 1), iota(shape3, 2)
    none = jnp.zeros((1, SIDE, C), F32)
    for p in range(NP):
        arrive(m2_copies[p])
        owner = owner_ref[p]
        from_x, from_z = (x - (owner >> 2)) & 3, (z - (owner & 3)) & 3
        blk[0:8] = m2_recv[p][0, from_x, 0:8]
        blk[8:16] = m2_recv[p][1, from_z, 0:8]
        clean = jnp.where(lane2 < SIDE, m2_recv[p][0, from_x, 8].astype(F32), 0.0)
        xcol = right.at[0]
        gcol = right.at[1]
        block = blk[...].astype(F32)
        for s, moved in enumerate(column_shifts(block)):
            rows = moved.astype(BF16)
            for r in range(3):
                store_rows(xcol, p, (3 * r + s) * C, rows, r - 1)

        level = jnp.full((SIDE, C), level_ref[p], jnp.int32).astype(F32)
        sigma = jnp.exp(LOG_LOW + level * LOG_STEP)
        variance = sigma * sigma + SIGMA_DATA * SIGMA_DATA
        scale_in = 1.0 / jnp.sqrt(variance)
        scale_skip = SIGMA_DATA * SIGMA_DATA / variance
        scale_out = sigma * SIGMA_DATA * scale_in
        embed = jnp.log(sigma) / 4.0
        noisy = clean + sigma * noise_v[p]
        aim = (clean - scale_skip * noisy) / scale_out
        scaled = pltpu.roll(scale_in * noisy, 1, axis=1)
        wide = jnp.broadcast_to(scaled[:, None, :], shape3)
        for bit in (1, 2, 4, 8):
            wide = jnp.where((col3 & bit) != 0, pltpu.roll(wide, C - bit, axis=2), wide)
        wide = jnp.where(lane3 < 3, wide, 0.0)
        taps = (
            jnp.concatenate([none, wide[: SIDE - 1]], axis=0)
            + pltpu.roll(wide, 3, axis=2)
            + pltpu.roll(jnp.concatenate([wide[1:], none], axis=0), 6, axis=2)
        )
        taps_hi = taps.astype(BF16).astype(F32)
        emb = embed[0:1, :][None]
        emb_hi = emb.astype(BF16).astype(F32)
        extra = taps_hi + pltpu.roll(taps_hi, 9, axis=2) + pltpu.roll(taps - taps_hi, 18, axis=2)
        extra = jnp.where((lane3 == 27) | (lane3 == 28), 1.0, extra)
        extra = jnp.where((lane3 == 29) | (lane3 == 30), emb_hi, extra)
        extra = jnp.where(lane3 == 31, emb - emb_hi, extra)
        xcol[p * SIDE : (p + 1) * SIDE, :, WIDE:] = extra.astype(BF16)

        cells = slice(p * CELLS, (p + 1) * CELLS)
        window = xcol[p * SIDE : (p + 1) * SIDE].reshape(CELLS, WIDE + C)
        pre_a = jnp.dot(window, wfull[...], preferred_element_type=F32)
        gate = jax.nn.sigmoid(pre_a)
        slope[...] = gate * (1.0 + pre_a * (1.0 - gate))
        hidden = (pre_a * gate).astype(BF16)
        left[1, cells] = hidden

        spread = jnp.dot(hidden, w2[...], preferred_element_type=F32).reshape(SIDE, SIDE, WIDE)

        def tap_rows(s):
            up = spread[:, :, s * C : (s + 1) * C]
            mid = spread[:, :, (3 + s) * C : (4 + s) * C]
            down = spread[:, :, (6 + s) * C : (7 + s) * C]
            return (
                mid
                + jnp.concatenate([none, up[: SIDE - 1]], axis=0)
                + jnp.concatenate([down[1:], none], axis=0)
            )

        before = jnp.where(col3 == 0, 0.0, pltpu.roll(tap_rows(0), 1, axis=1))
        after = jnp.where(col3 == SIDE - 1, 0.0, pltpu.roll(tap_rows(2), SIDE - 1, axis=1))
        pre_b = bb + tap_rows(1) + before + after
        gate_b = jax.nn.sigmoid(pre_b)
        aim3 = jnp.where(col3 == lane3, jnp.broadcast_to(aim[:, None, :], shape3), 0.0)
        residual = jnp.sum(pre_b * gate_b * wo - aim3, axis=2, keepdims=True)
        weight = count_ref[p].astype(F32)
        losses_ref[p] = jnp.sum(residual * residual) * weight / CELLS
        grad_final = (2.0 * weight / CELLS) * residual
        grad_b = grad_final * wo * (gate_b * (1.0 + pre_b * (1.0 - gate_b)))
        grad_b = grad_b.astype(BF16).astype(F32)
        raw_send[p] = jnp.where(core == 0, grad_b, block).astype(BF16)
        for s, moved in enumerate(column_shifts(grad_b)):
            rows = moved.astype(BF16)
            for r in range(3):
                store_rows(gcol, p, (3 * (2 - r) + (2 - s)) * C, rows, r - 1)

        back = lax.dot_general(
            gcol[p * SIDE : (p + 1) * SIDE, :, 0:WIDE].reshape(CELLS, WIDE),
            w2[...],
            (((1,), (1,)), ((), ())),
            preferred_element_type=F32,
        )
        left[0, cells] = (back * slope[...]).astype(BF16)

        row = []
        for i, src, dst in (
            (0, raw_send.at[p], raw_recv.at[p]),
            (
                1,
                left.at[1 - core, pl.ds(p * CELLS, CELLS)],
                left.at[1 - core, pl.ds((NP + p) * CELLS, CELLS)],
            ),
        ):
            copy = remote(
                src, dst, sib_ssem.at[2 * p + i], sib_rsem.at[2 * p + i], me_t, sib
            )
            copy.start()
            row.append(copy)
        pair_copies.append(row)

    def sibling_columns(p):
        arrive(pair_copies[p])
        dst = right.at[core]
        for s, moved in enumerate(column_shifts(raw_recv[p].astype(F32))):
            rows = moved.astype(BF16)
            for r in range(3):
                tap = 3 * r + s
                lane = pl.multiple_of(jnp.where(core == 0, tap, TAPS - 1 - tap) * C, C)
                store_rows(dst, NP + p, lane, rows, r - 1)

    for p in range(NP - 1):
        sibling_columns(p)

    def gradient(tile, tiles, first, count):
        return lax.dot_general(
            left[core, first * CELLS : (first + count) * CELLS],
            right[
                core, first * SIDE : (first + count) * SIDE, :, tile * C : (tile + tiles) * C
            ].reshape(count * CELLS, tiles * C),
            (((0,), (0,)), ((), ())),
            preferred_element_type=F32,
        )

    def along(axis, o):
        if axis == 0:
            at = (x + o) & 3
            return (at << 2) | z, me_d, at
        if axis == 1:
            at = (z + o) & 3
            return (x << 2) | at, me_d, at
        at = (y + o) & 3
        return me_t, (at << 1) | core, at

    here = (x, z, y)
    orders = ((0, 1, 2), (1, 2, 0), (2, 0, 1))

    def piece1(chunk, part, at):
        lanes = slice(part * C, (part + 1) * C)
        if part == 0:
            return mine[chunk, at, :, :, :, lanes]
        if part == 1:
            return mine[chunk, :, at, :, :, lanes]
        return mine[chunk, :, :, at, :, lanes]

    s1_copies = [[], [], []]

    def put(tile, tiles, total, more):
        total = total.reshape(AX, AX, AX, 8, tiles * C)
        for i in range(tiles):
            chunk, part = (tile + i) // 3, (tile + i) % 3
            at = (chunk, slice(None), slice(None), slice(None), slice(None))
            at = at + (slice(part * C, (part + 1) * C),)
            piece = total[..., i * C : (i + 1) * C]
            mine[at] = mine[at] + piece if more else piece

    def step1(chunk):
        for o in (2, 1, 3):
            for part in range(3):
                tile, dp, at = along(orders[part][0], o)
                n = chunk * 9 + part * 3 + o - 1
                s1_send[n] = piece1(chunk, part, at).reshape(128, C).astype(BF16)
                copy = remote(
                    s1_send.at[n], s1_recv.at[n], s1_ssem.at[n], s1_rsem.at[n], tile, dp
                )
                copy.start()
                s1_copies[part].append(copy)

    last = 2 * NP - 1
    put(0, 4, gradient(0, 4, 0, last), False)
    put(4, 2, gradient(4, 2, 0, last), False)
    sibling_columns(NP - 1)
    put(0, 4, gradient(0, 4, last, 1), True)
    step1(0)
    put(4, 2, gradient(4, 2, last, 1), True)
    step1(1)
    put(6, 3, gradient(6, 3, 0, last + 1), False)
    step1(2)

    def piece2(part, at):
        return tot2[part, :, at] if part == 1 else tot2[part, at]

    s2_copies = []
    for part in range(3):
        arrive(s1_copies[part])
        for chunk in range(3):
            total = piece1(chunk, part, here[orders[part][0]])
            for o in range(3):
                landed = s1_recv[chunk * 9 + part * 3 + o].astype(F32)
                total = total + landed.reshape(AX, AX, 8, C)
            tot2[part, :, :, :, chunk * C : (chunk + 1) * C] = total
        row = []
        for o in (2, 1, 3):
            tile, dp, at = along(orders[part][1], o)
            n = part * 3 + o - 1
            s2_send[n] = piece2(part, at).reshape(32, PART).astype(BF16)
            copy = remote(s2_send.at[n], s2_recv.at[n], s2_ssem.at[n], s2_rsem.at[n], tile, dp)
            copy.start()
            row.append(copy)
        s2_copies.append(row)

    settle()

    s3_copies = []
    for part in range(3):
        arrive(s2_copies[part])
        total = piece2(part, here[orders[part][1]])
        for o in range(3):
            total = total + s2_recv[part * 3 + o].astype(F32).reshape(AX, 8, PART)
        tot3[part] = total
        row = []
        for o in (2, 1, 3):
            tile, dp, at = along(orders[part][2], o)
            n = part * 3 + o - 1
            copy = remote(
                tot3.at[part, at], s3_recv.at[n], s3_ssem.at[n], s3_rsem.at[n], tile, dp
            )
            copy.start()
            row.append(copy)
        s3_copies.append(row)

    settle()
    squares = jnp.zeros((8, C), F32)
    for part in range(3):
        arrive(s3_copies[part])
        total = tot3[part, here[orders[part][2]]]
        for o in range(3):
            total = total + s3_recv[part * 3 + o]
        for i in range(3):
            piece = total[:, i * C : (i + 1) * C]
            fin[0, :, (3 * i + part) * C : (3 * i + part + 1) * C] = piece
            squares = squares + piece * piece

    nrm_send[...] = squares
    nrm_recv[0] = squares
    copies = []
    for o in range(1, N_TILE):
        copy = remote(nrm_send, nrm_recv.at[o], n1_ssem.at[o], n1_rsem.at[o], tile_peer(o), me_d)
        copy.start()
        copies.append(copy)
    fin_copy = remote(fin.at[0], fin.at[1], fin_sem.at[0], fin_sem.at[1], me_t, sib)
    fin_copy.start()
    settle()
    arrive(copies)
    plane = jnp.sum(nrm_recv[...], axis=0)
    nrm2_send[...] = plane
    nrm2_recv[me_d] = plane
    copies = []
    for o in range(1, N_DP):
        copy = remote(
            nrm2_send, nrm2_recv.at[me_d], n2_ssem.at[o], n2_rsem.at[o], me_t, dp_peer(o)
        )
        copy.start()
        copies.append(copy)
    settle()
    arrive([fin_copy, *copies])
    settle()

    total_a = jnp.sum(nrm2_recv[0] + nrm2_recv[2] + nrm2_recv[4] + nrm2_recv[6], keepdims=True)
    total_b = jnp.sum(nrm2_recv[1] + nrm2_recv[3] + nrm2_recv[5] + nrm2_recv[7], keepdims=True)
    root_a = jnp.sqrt(total_a / (HID * WIDE) + EPSILON)
    root_b = jnp.sqrt(total_b / (HID * WIDE) + EPSILON)
    full_a = fin[core] / root_a
    full_b = fin[1 - core] / root_b
    first = core == 0
    upda_ref[...] = jnp.where(first, full_a[0:4], full_a[4:8])
    updb_ref[...] = jnp.where(first, full_b[0:4], full_b[4:8])


def leave(a_in, b_in, c_in, a_out, b_out, c_out, sem):
    pairs = ((a_in, a_out), (b_in, b_out), (c_in, c_out))
    copies = [pltpu.make_async_copy(s, d, sem.at[i]) for i, (s, d) in enumerate(pairs)]
    for copy in copies:
        copy.start()
    for copy in copies:
        copy.wait()


def local(features, target_field, owner_tile, *rest):
    vmem = pl.BlockSpec(memory_space=pltpu.VMEM)
    smem = pl.BlockSpec(memory_space=pltpu.SMEM)
    hbm = pl.BlockSpec(memory_space=pl.ANY)
    dma = pltpu.SemaphoreType.DMA
    ints = pltpu.SMEM((NP,), jnp.int32)
    scratch = [
        ints,
        ints,
        ints,
        ints,
        ints,
        pltpu.VMEM((64, 256, C), BF16),
        pltpu.VMEM((64, 256, C), F32),
        pltpu.VMEM((64, 256), BF16),
        pltpu.VMEM((2, 64, C), F32),
        pltpu.VMEM((NP, SIDE, SIDE), F32),
        pltpu.VMEM((NP, SIDE, C), F32),
        pltpu.VMEM((TAPS, HID), F32),
        pltpu.VMEM((HID,), F32),
        pltpu.VMEM((HID,), F32),
        pltpu.VMEM((C,), F32),
        pltpu.VMEM((C,), F32),
        pltpu.VMEM((1, C), jnp.int32),
        pltpu.VMEM((N_TILE, 1, C), jnp.int32),
        pltpu.SMEM((N_TILE, 1, C), jnp.int32),
        pltpu.VMEM((6, 65, SIDE, C), BF16),
        pltpu.VMEM((2, AX, 65, SIDE, C), BF16),
        pltpu.VMEM((8, NP, 9, SIDE, C), BF16),
        pltpu.VMEM((2, AX, 9, SIDE, C), BF16),
        pltpu.VMEM((2, AX, 9, SIDE, C), BF16),
        pltpu.VMEM((2, AX, 9, SIDE, C), BF16),
        pltpu.VMEM((2, AX, 9, SIDE, C), BF16),
        pltpu.VMEM((SIDE, SIDE, C), BF16),
        pltpu.VMEM((WIDE + C, HID), BF16),
        pltpu.VMEM((C, HID), F32),
        pltpu.VMEM((HID, WIDE), BF16),
        pltpu.VMEM((2, 2 * NP * CELLS, HID), BF16),
        pltpu.VMEM((2, 2 * NP * SIDE, SIDE, WIDE + C), BF16),
        pltpu.VMEM((CELLS, HID), F32),
        pltpu.VMEM((NP, SIDE, SIDE, C), BF16),
        pltpu.VMEM((NP, SIDE, SIDE, C), BF16),
        pltpu.VMEM((3, AX, AX, AX, 8, PART), F32),
        pltpu.VMEM((27, 128, C), BF16),
        pltpu.VMEM((27, 128, C), BF16),
        pltpu.VMEM((3, AX, AX, 8, PART), F32),
        pltpu.VMEM((9, 32, PART), BF16),
        pltpu.VMEM((9, 32, PART), BF16),
        pltpu.VMEM((3, AX, 8, PART), F32),
        pltpu.VMEM((9, 8, PART), F32),
        pltpu.VMEM((2, 8, WIDE), F32),
        pltpu.VMEM((8, C), F32),
        pltpu.VMEM((N_TILE, 8, C), F32),
        pltpu.VMEM((8, C), F32),
        pltpu.VMEM((N_DP, 8, C), F32),
        dma((32,)),
        dma((N_TILE,)),
        dma((N_TILE,)),
        dma((6,)),
        dma((6,)),
        dma((32,)),
        dma((32,)),
        dma((2 * NP,)),
        dma((2 * NP,)),
        dma((27,)),
        dma((27,)),
        dma((9,)),
        dma((9,)),
        dma((9,)),
        dma((9,)),
        dma((2,)),
        dma((N_TILE,)),
        dma((N_TILE,)),
        dma((N_DP,)),
        dma((N_DP,)),
    ]
    outs = (
        jax.ShapeDtypeStruct((NP,), F32),
        jax.ShapeDtypeStruct((4, WIDE), F32),
        jax.ShapeDtypeStruct((4, WIDE), F32),
    )
    results = pl.pallas_call(
        kernel,
        out_shape=(outs[0], pltpu.VMEM((4, WIDE), F32), pltpu.VMEM((4, WIDE), F32)),
        in_specs=[hbm] * 15,
        out_specs=(smem, vmem, vmem),
        scratch_shapes=scratch,
        compiler_params=pltpu.CompilerParams(
            collective_id=0, has_side_effects=True, vmem_limit_bytes=60 * 2**20
        ),
    )(features, target_field, owner_tile.reshape(-1), *rest)
    return pl.pallas_call(
        leave,
        out_shape=outs,
        in_specs=[hbm, vmem, vmem],
        out_specs=(hbm,) * 3,
        scratch_shapes=[dma((3,))],
    )(results[0], *[pltpu.with_memory_space_constraint(a, pltpu.VMEM) for a in results[1:]])


def solution(mesh):
    both = ("tile", "dp")
    return jax.shard_map(
        local,
        mesh=mesh,
        in_specs=(
            P("tile", None, None),
            P("tile", None),
            P(both, None),
            P(both),
            P(both),
            P(both),
            P(both),
            P(both, None, None),
            P(),
            P(),
            P(),
            P(),
            P(),
            P(),
            P(),
        ),
        out_specs=(P(both), P(both, None), P(both, None)),
        check_vma=False,
    )
```
